32 devices in a mesh: groups: 2 (over x), expert: 8 (over z, y), sub: 2 (over core).
Axes of the slice: x: 2, y: 2, z: 4, core: 2. Of those that a mesh axis runs over, the one named last changes fastest.
Arguments:
- hidden_state: bfloat16 [2048, 2048], P(('groups', 'expert', 'sub')), parts along dimension 0, may hold values from -6 to 6
- norm_gain: float32 [2048], replicated, may hold values from 0.5 to 1.5
- router_weight: bfloat16 [2048, 16], replicated, may hold values from -0.25 to 0.25
- expert_ids: int32 [2048, 6], P(('groups', 'expert', 'sub')), parts along dimension 0, may hold values from 0 to 15, all different within a row; in each aligned block of 64 rows (0 to 63, 64 to 127, ...) at most 32 rows name the same one
- live_counts: int32 [32], P(('groups', 'expert', 'sub')), parts along dimension 0, may hold values from 16 to 64
- routed_gate_up: bfloat16 [16, 2048, 2816], P(('expert', 'sub')), may hold values from -0.125 to 0.125
- routed_down: bfloat16 [16, 1408, 2048], P(('expert', 'sub')), may hold values from -0.15625 to 0.15625
- shared_weights: bfloat16 [3, 2048, 2816], P(None, None, 'expert'), may hold values from -0.125 to 0.125
Outputs:
- mixed: bfloat16 [2048, 2048], P(('groups', 'expert', 'sub')), parts along dimension 0
- penalty: float32 [2], P('groups'), parts along dimension 0
The draws below stay inside these ranges and needn't reach their ends.
There are 2 independent parts, one for each index of `groups`. The reference program is written for one: setup_inputs(seed, part) draws one part's arguments, and reference() takes and returns one part's arrays. A program takes and returns all parts, laid end to end along the dimension named above; an argument that names none is the same for every part. Nothing has to cross between parts.
Inputs may be any that keep to these rules, and one draw needn't show every extreme that they name: `expert_ids`: in each row the 6 experts differ; among the 64 rows of one device no expert is named more than 32 times.
All inputs are finite; a program needn't handle non-finite values.
Results may differ from the reference program's by a relative error of at most 0.0065.
Values may be sent and summed in bfloat16 or wider, within the bound.
No kernel may reach another device: no remote copies, remote signals or barrier semaphores. Data moves between devices by JAX's collectives and lax.ppermute only.
A program may use at most 128 MiB of HBM per device.

```python
import math
import jax
import jax.numpy as jnp
import numpy as np
from jax import lax

D = 2048
FF = 1408
SHARED_FF = 2816
TOP = 6
TOK_DEV = 64
EXPERTS = 16
CAP = 32
TOKENS = 1024
N_EXPERT = 8
N_SUB = 2


def draw_live_counts(key, part):
    count = N_EXPERT * N_SUB
    lowest = max(TOK_DEV // 4, 1)
    spread = max(TOK_DEV // 8, 1)
    index = jnp.arange(count, dtype=jnp.int32)
    base = lowest + (TOK_DEV - lowest) * index // (count - 1)
    jitter = jax.random.randint(jax.random.fold_in(key, 17), (count,), -spread, spread + 1, dtype=jnp.int32)
    inner = ((index > 0) & (index < count - 1)).astype(jnp.int32)
    return jnp.clip(base + jitter * inner, lowest, TOK_DEV).astype(jnp.int32)


def level_of(rng, shape, cuts, low, largest):
    gain = 1.0
    for axis_at, blocks in cuts:
        heights = jax.random.uniform(jax.random.fold_in(jax.random.fold_in(rng, 6), axis_at), (blocks,), jnp.float32, low / len(cuts), largest / len(cuts))
        gain = gain * jnp.repeat(jnp.exp(heights), shape[axis_at] // blocks).reshape((-1,) + (1,) * (len(shape) - 1 - axis_at))
    return gain


def deal_out(key, own, number, rows, amount, top, limit, lean):
    order = jax.random.permutation(key, amount)
    crowded, ordinary = portions_of(amount, rows * top, limit, lean, True), portions_of(amount, rows * top, limit, lean, False)
    places = jnp.arange(amount)

    def named(sizes, rotation):
        used = int((sizes > 0).sum())
        fixed = max(1, used // 4)
        moved = fixed + (places - fixed + rotation * (used - fixed)) % max(1, amount - fixed)
        return jnp.zeros((amount,), jnp.int32).at[order[jnp.where(places < fixed, places, moved)]].set(jnp.asarray(sizes, jnp.int32))

    sizes = jnp.where(number % 4 == 0, named(crowded, number // 4), named(ordinary, number - number // 4 - 1))
    mixed = jax.random.permutation(jax.random.fold_in(own, 3), amount)
    donor, receiver = mixed[0:amount // 2 * 2:2], mixed[1:amount // 2 * 2:2]
    margin = jnp.minimum(sizes[donor] - 1, limit - sizes[receiver]) // 2
    margin = jnp.where((donor == order[0]) | (receiver == order[0]) | (sizes[receiver] == 0), 0, jnp.maximum(margin, 0))
    moved = jax.random.randint(jax.random.fold_in(own, 4), (amount // 2,), 0, 1 << 20) % (margin + 1)
    sizes = sizes.at[donor].add(-moved).at[receiver].add(moved)
    items = jnp.searchsorted(jnp.cumsum(sizes), jnp.arange(rows * top), side="right").astype(jnp.int32)
    listing = items.reshape(top, rows).T
    listing = listing[jax.random.permutation(jax.random.fold_in(own, 1), rows)]
    rotation = jax.random.randint(jax.random.fold_in(own, 2), (rows, 1), 0, top)
    return jnp.take_along_axis(listing, (jnp.arange(top)[None, :] + rotation) % top, axis=1)


def portions_of(count, total, bound, lean, full):
    loads = [(1 << 20) // math.isqrt(rank ** lean) + 1 for rank in range(1, count + 1)]
    largest = bound if full else min(bound, max(-(-total // count), total * loads[0] // sum(loads)))
    least = 1 if total - largest >= count - 1 else 0
    counts, rest = [largest] + [least] * (count - 1), total - largest - least * (count - 1)
    while rest > 0:
        candidates = [i for i in range(1, count) if counts[i] < largest] or [i for i in range(1, count) if counts[i] < bound]
        pool, left = sum([loads[i] for i in candidates]), rest
        for i in candidates:
            extra = min(bound - counts[i], max(1, left * loads[i] // pool), rest)
            counts[i] = counts[i] + extra
            rest = rest - extra
    return np.array(counts)


def scatter_about(stream_key, extent, scale, most, cuts=(), kind=jnp.bfloat16):
    level = level_of(stream_key, extent, cuts, -0.22, 0.18) if cuts else 1.0
    entries = jax.random.normal(stream_key, extent, jnp.float32) * scale * level
    return jnp.minimum(jnp.maximum(entries, -most), most).astype(kind)


def setup_inputs(seed: int = 0, part: int = 0) -> dict:
    keys = jax.random.split(jax.random.key(seed), 9)
    own_keys = jax.random.split(jax.random.fold_in(keys[8], part), 9)
    hidden_state = scatter_about(own_keys[0], (TOKENS, D), 1.0, 6.0, ((0, 16),))
    norm_gain = jnp.clip(1.0 + 0.1 * jax.random.normal(keys[1], (D,), jnp.float32), 0.5, 1.5)
    router_weight = scatter_about(keys[2], (D, EXPERTS), (D // 4) ** -0.5, 0.25)
    expert_ids_keys = jax.random.split(jax.random.fold_in(own_keys[3], 1), TOKENS // TOK_DEV)
    expert_ids_turns = jax.random.permutation(jax.random.fold_in(own_keys[3], 3), TOKENS // TOK_DEV)
    expert_ids = jax.vmap(lambda own, number: deal_out(jax.random.fold_in(own_keys[3], 2), own, number, TOK_DEV, EXPERTS, TOP, CAP, 1))(expert_ids_keys, expert_ids_turns).reshape((TOKENS, TOP))
    live_counts = draw_live_counts(jax.random.fold_in(jax.random.fold_in(keys[8], part), 71), part)
    routed_gate_up = scatter_about(keys[5], (EXPERTS, D, 2 * FF), D ** -0.5, 0.125, ((0, 16),))
    routed_down = scatter_about(keys[6], (EXPERTS, FF, D), FF ** -0.5, 0.15625, ((0, 16),))
    shared_weights = scatter_about(keys[7], (3, D, SHARED_FF), D ** -0.5, 0.125, ((2, 8),))
    return {"hidden_state": hidden_state, "norm_gain": norm_gain, "router_weight": router_weight, "expert_ids": expert_ids, "live_counts": live_counts, "routed_gate_up": routed_gate_up, "routed_down": routed_down, "shared_weights": shared_weights}


def normalize(states, norm_gain):
    values = states.astype(jnp.float32)
    spread = lax.optimization_barrier(jnp.mean(values * values, axis=-1, keepdims=True))
    return (values * lax.rsqrt(spread + 1e-06) * norm_gain).astype(jnp.bfloat16)

def expert_ffn(packed):
    inputs, gate_up, down_proj = packed
    inner = jnp.dot(inputs, gate_up, preferred_element_type=jnp.float32)
    active = (jax.nn.silu(inner[:, :FF]) * inner[:, FF:]).astype(jnp.bfloat16)
    return jnp.dot(active, down_proj, preferred_element_type=jnp.float32).astype(jnp.bfloat16)

def reference(hidden_state, norm_gain, router_weight, expert_ids, live_counts, routed_gate_up, routed_down, shared_weights):
    devices = N_EXPERT * N_SUB
    normed = normalize(hidden_state, norm_gain)
    probs = jax.nn.sigmoid(jnp.dot(normed, router_weight, preferred_element_type=jnp.float32))
    positions = jnp.arange(TOKENS, dtype=jnp.int32)
    owners = positions // TOK_DEV
    live = (positions % TOK_DEV < live_counts[owners]).astype(jnp.float32)
    columns = jnp.arange(EXPERTS, dtype=jnp.int32)
    onehot = (expert_ids[:, :, None] == columns[None, None, :]).astype(jnp.int32)
    picked = lax.optimization_barrier(jnp.sum(onehot.astype(jnp.float32) * probs[:, None, :], axis=-1))
    weights = (live[:, None] * picked / lax.optimization_barrier(jnp.sum(picked, axis=-1, keepdims=True))).astype(jnp.bfloat16)
    live_hot = onehot * live.astype(jnp.int32)[:, None, None]
    per_device = live_hot.reshape(devices, TOK_DEV * TOP, EXPERTS)
    ranks = jnp.cumsum(per_device, axis=1) - per_device
    slot = lax.optimization_barrier(jnp.sum(ranks * per_device, axis=-1)).reshape(devices, TOK_DEV, TOP)
    places = expert_ids.reshape(devices, TOK_DEV, TOP) * CAP + slot
    valid = live.reshape(devices, TOK_DEV, 1, 1)
    cells = jnp.arange(EXPERTS * CAP, dtype=jnp.int32)
    match = (places[..., None] == cells[None, None, None, :]).astype(jnp.float32)
    table = lax.optimization_barrier(jnp.sum(match, axis=2)) * valid[:, :, 0]
    buffer = jnp.einsum('dtc,dtf->dcf', table, normed.reshape(devices, TOK_DEV, D).astype(jnp.float32)).astype(jnp.bfloat16)
    buffer = buffer.reshape(devices, EXPERTS, CAP, D).transpose(1, 0, 2, 3).reshape(EXPERTS, devices * CAP, D)
    outputs = lax.map(expert_ffn, (buffer, routed_gate_up, routed_down))
    outputs = outputs.reshape(EXPERTS, devices, CAP, D).transpose(1, 0, 2, 3).reshape(devices, EXPERTS * CAP, D)
    mixing = lax.optimization_barrier(jnp.sum(match * weights.reshape(devices, TOK_DEV, TOP, 1).astype(jnp.float32), axis=2))
    routed = jnp.einsum('dtc,dcf->dtf', mixing, outputs.astype(jnp.float32)).reshape(TOKENS, D)
    gate_part = jnp.dot(normed, shared_weights[0], preferred_element_type=jnp.float32)
    up_part = jnp.dot(normed, shared_weights[1], preferred_element_type=jnp.float32)
    shared_active = (jax.nn.silu(gate_part) * up_part).astype(jnp.bfloat16)
    shared_out = lax.dot_general(shared_active, shared_weights[2], (((1,), (1,)), ((), ())), preferred_element_type=jnp.float32)
    mixed = (shared_out + routed).astype(jnp.bfloat16)
    load = lax.optimization_barrier(jnp.sum(live_hot.astype(jnp.float32), axis=(0, 1)))
    mass = lax.optimization_barrier(jnp.sum(probs * live[:, None], axis=0))
    penalty = EXPERTS * jnp.sum(load * mass) / (TOP * float(TOKENS) * float(TOKENS))
    return (mixed, penalty.reshape(1))
```

```python
import jax
import jax.numpy as jnp
from jax import lax
from jax.sharding import PartitionSpec as P


F32 = jnp.float32
BF16 = jnp.bfloat16


def normalize(states, norm_gain):
    values = states.astype(F32)
    spread = jnp.mean(values * values, axis=-1, keepdims=True)
    return (values * lax.rsqrt(spread + 1e-06) * norm_gain).astype(BF16)


def split_three(values):
    high = lax.reduce_precision(values, 8, 7)
    middle = lax.reduce_precision(values - high, 8, 7)
    low = values - high - middle
    return high.astype(BF16), middle.astype(BF16), low.astype(BF16)


def on_device(
    hidden_state,
    norm_gain,
    router_weight,
    expert_ids,
    live_counts,
    routed_gate_up,
    routed_down,
    shared_weights,
):
    tok_rows, width = hidden_state.shape
    choose = expert_ids.shape[1]
    hidden_units = routed_down.shape[1]
    expert_count = lax.axis_size("expert")
    sub_count = lax.axis_size("sub")
    devices = expert_count * sub_count
    all_experts = routed_gate_up.shape[0] * devices
    assert routed_gate_up.shape[0] == 1 and sub_count == 2
    all_tokens = tok_rows * devices
    capacity = (tok_rows * choose * 4 + 3 * all_experts - 1) // (3 * all_experts)
    me = lax.axis_index("expert") * sub_count + lax.axis_index("sub")

    def cross(block, step):
        return lax.ppermute(block, "expert", [(e, e ^ step) for e in range(expert_count)])

    def swap(block):
        return lax.ppermute(block, "sub", [(0, 1), (1, 0)])

    normed = normalize(hidden_state, norm_gain)
    probs = jax.nn.sigmoid(jnp.dot(normed, router_weight, preferred_element_type=F32))
    live = (jnp.arange(tok_rows, dtype=jnp.int32) < live_counts[0]).astype(F32)
    columns = jnp.arange(all_experts, dtype=jnp.int32)
    named = jnp.sum((expert_ids[:, :, None] == columns[None, None, :]).astype(F32), axis=1)
    picked = named * probs
    weights = (live[:, None] * picked / jnp.sum(picked, axis=-1, keepdims=True)).astype(BF16)
    taken = named * live[:, None]
    earlier = (
        jnp.arange(tok_rows)[:, None] > jnp.arange(tok_rows)[None, :]
    ).astype(BF16)
    slot = jnp.dot(earlier, taken.astype(BF16), preferred_element_type=F32)
    code = (taken * (slot + 1.0)).astype(BF16)
    load = jnp.sum(taken, axis=0, keepdims=True)
    mass = jnp.sum(probs * live[:, None], axis=0, keepdims=True)
    sums = jnp.concatenate([load.astype(BF16), *split_three(mass)], axis=1)
    sums = jnp.broadcast_to(sums, (tok_rows, sums.shape[1]))
    meta = jnp.concatenate([weights, code, sums], axis=1)
    lanes = -(-meta.shape[1] // 128) * 128
    meta = jnp.pad(meta, ((0, 0), (0, lanes - meta.shape[1])))
    packet = jnp.concatenate([normed, meta], axis=1)

    half = max(expert_count // 4, 1)
    steps = expert_count // 2
    chunks = [range(0, half), range(half, steps)]
    direct = [packet] + [cross(packet, 2 * j) for j in range(1, steps)]

    mine = (columns == me).astype(F32)
    slots = jnp.arange(capacity, dtype=jnp.int32).astype(F32) + 1.0
    gate_up, down = routed_gate_up[0], routed_down[0]
    device_sums = {}
    chip_parts = {}
    for chunk in chunks:
        blocks = []
        for j in chunk:
            blocks += [direct[j], cross(direct[j], 1)]
        own = jnp.concatenate(blocks, axis=0)
        other = swap(own)
        count = len(blocks)
        tokens = jnp.concatenate([own, other], axis=0)
        notes = tokens[:, width:].astype(F32)
        for side in range(2):
            for i, k in enumerate([2 * j + b for j in chunk for b in range(2)]):
                device_sums[2 * k + side] = notes[(side * count + i) * tok_rows, 2 * all_experts :]
        scale = jnp.sum(notes[:, :all_experts] * mine, axis=1).reshape(2 * count, tok_rows)
        place = jnp.sum(notes[:, all_experts : 2 * all_experts] * mine, axis=1)
        place = place.reshape(2 * count, tok_rows)
        states = tokens[:, :width].reshape(2 * count, tok_rows, width)
        match = (place[:, :, None] == slots[None, None, :]).astype(F32)
        rows = jnp.einsum(
            "btc,btd->bcd", match.astype(BF16), states, preferred_element_type=F32
        ).astype(BF16)
        rows = rows.reshape(2 * count * capacity, width)
        inner = jnp.dot(rows, gate_up, preferred_element_type=F32)
        active = (jax.nn.silu(inner[:, :hidden_units]) * inner[:, hidden_units:]).astype(BF16)
        results = jnp.dot(active, down, preferred_element_type=F32).astype(BF16)
        results = results.reshape(2 * count, capacity, width)
        mixing = (match * scale[:, :, None]).astype(BF16)
        routed = jnp.einsum("btc,bcd->btd", mixing, results, preferred_element_type=F32)
        arrived = swap(routed[count:].astype(BF16))
        states = own[:, :width]
        gate_part = jnp.dot(states, shared_weights[0], preferred_element_type=F32)
        up_part = jnp.dot(states, shared_weights[1], preferred_element_type=F32)
        shared_active = (jax.nn.silu(gate_part) * up_part).astype(BF16)
        partials = lax.dot_general(
            shared_active, shared_weights[2], (((1,), (1,)), ((), ())), preferred_element_type=F32
        ).reshape(count, tok_rows, width)
        total = partials + routed[:count] + arrived.astype(F32)
        for i, k in enumerate([2 * j + b for j in chunk for b in range(2)]):
            chip_parts[k] = total[i]

    mixed = None
    for j in reversed(range(steps)):
        pair = chip_parts[2 * j] + cross(chip_parts[2 * j + 1].astype(BF16), 1).astype(F32)
        term = pair if j == 0 else cross(pair.astype(BF16), 2 * j).astype(F32)
        mixed = term if mixed is None else mixed + term
    mixed = mixed.astype(BF16)

    table = jnp.stack([device_sums[r] for r in range(devices)])
    order = (jnp.arange(devices)[:, None] == (jnp.arange(devices)[None, :] ^ me)).astype(F32)
    table = jnp.sum(order[:, :, None] * table[None, :, :], axis=1)
    parts = table[:, : 4 * all_experts].reshape(devices, 4, all_experts)
    load = jnp.sum(parts[:, 0], axis=0)
    mass = jnp.sum((parts[:, 1] + parts[:, 2]) + parts[:, 3], axis=0)
    penalty = all_experts * jnp.sum(load * mass) / (choose * float(all_tokens) * float(all_tokens))
    return (mixed, penalty.reshape(1))


def solution(mesh):
    placed = (
        P(("groups", "expert", "sub"), None),
        P(),
        P(),
        P(("groups", "expert", "sub"), None),
        P(("groups", "expert", "sub")),
        P(("expert", "sub"), None, None),
        P(("expert", "sub"), None, None),
        P(None, None, "expert"),
    )
    return jax.shard_map(
        on_device,
        mesh=mesh,
        in_specs=placed,
        out_specs=(P(("groups", "expert", "sub"), None), P("groups")),
        check_vma=False,
    )
```

```python
import functools

import jax
import jax.numpy as jnp
from jax import lax
from jax.experimental import pallas as pl
from jax.experimental.pallas import tpu as pltpu
from jax.sharding import PartitionSpec as P


F32 = jnp.float32
BF16 = jnp.bfloat16
VMEM = pl.BlockSpec(memory_space=pltpu.VMEM)
SMEM = pl.BlockSpec(memory_space=pltpu.SMEM)
ANY = pl.BlockSpec(memory_space=pl.ANY)


def split_three(values):
    high = values.astype(BF16)
    rest = values - high.astype(F32)
    middle = rest.astype(BF16)
    low = (rest - middle.astype(F32)).astype(BF16)
    return high, middle, low


def iota(shape, axis):
    return lax.broadcasted_iota(jnp.int32, shape, axis)


def route_kernel(live_ref, hidden_ref, gain_ref, router_ref, ids_ref, packet_ref):
    rows, width = hidden_ref.shape
    experts = router_ref.shape[1]
    lanes = packet_ref.shape[1] - width
    values = hidden_ref[...].astype(F32)
    spread = jnp.mean(values * values, axis=-1, keepdims=True)
    normed = (values * lax.rsqrt(spread + 1e-06) * gain_ref[...]).astype(BF16)
    packet_ref[:, :width] = normed
    logits = jnp.dot(normed, router_ref[...], preferred_element_type=F32)
    probs = 1.0 / (1.0 + jnp.exp(-logits))
    live = (iota((rows, 1), 0) < live_ref[0]).astype(F32)
    columns = iota((rows, experts), 1)
    named = jnp.zeros((rows, experts), F32)
    for k in range(ids_ref.shape[1]):
        named = named + (ids_ref[:, k : k + 1] == columns).astype(F32)
    picked = named * probs
    weights = (live * picked / jnp.sum(picked, axis=-1, keepdims=True)).astype(BF16)
    taken = named * live
    earlier = (iota((rows, rows), 0) > iota((rows, rows), 1)).astype(BF16)
    slot = jnp.dot(earlier, taken.astype(BF16), preferred_element_type=F32)
    code = (taken * (slot + 1.0)).astype(BF16)
    load = jnp.sum(taken, axis=0, keepdims=True).astype(BF16)
    mass = jnp.sum(probs * live, axis=0, keepdims=True)
    meta = jnp.zeros((rows, lanes), F32)
    for at, piece in enumerate([weights, code, load, *split_three(mass)]):
        put = (iota((experts, lanes), 1) == iota((experts, lanes), 0) + at * experts).astype(BF16)
        piece = jnp.broadcast_to(piece, (rows, experts))
        meta = meta + jnp.dot(piece, put, preferred_element_type=F32)
    packet_ref[:, width:] = meta.astype(BF16)


def columns_of(block_ref, width, at):
    notes = block_ref[:, width:].astype(F32)
    lane = iota(notes.shape, 1)
    return [jnp.sum(jnp.where(lane == a, notes, 0.0), axis=1, keepdims=True) for a in at]


def matches(block_ref, width, experts, capacity, me, peer):
    rows = block_ref.shape[0]
    mine, theirs = columns_of(block_ref, width, [experts + me, experts + peer])
    slot = iota((rows, 2 * capacity), 1)
    place = jnp.where(slot < capacity, mine, theirs).astype(jnp.int32)
    return (place - 1) == jnp.where(slot < capacity, slot, slot - capacity), slot


def pick_kernel(count, width, experts, capacity, me_ref, *refs):
    blocks, (mine_ref, peer_ref) = refs[:count], refs[count:]
    me = me_ref[0]
    peer = me_ref[1]
    for i, block in enumerate(blocks):
        match, _ = matches(block, width, experts, capacity, me, peer)
        rows = lax.dot_general(
            match.astype(F32).astype(BF16),
            block[:, :width],
            (((0,), (0,)), ((), ())),
            preferred_element_type=F32,
        ).astype(BF16)
        mine_ref[i * capacity : (i + 1) * capacity, :] = rows[:capacity]
        peer_ref[i * capacity : (i + 1) * capacity, :] = rows[capacity:]


def silu(value):
    return value / (1.0 + jnp.exp(-value))


def expert_kernel(
    mine_ref, peer_ref, up_hbm, down_hbm, mine_out, peer_out, up, down, active, up_sem, down_sem
):
    half = mine_ref.shape[0]
    width = mine_ref.shape[1]
    units = down_hbm.shape[0]
    tiles = units // 128
    parts = down.shape[0]
    wide = width // parts
    copies = []
    for t in range(tiles):
        pair = []
        for s in range(2):
            at = pl.ds(s * units + t * 128, 128)
            pair.append(pltpu.make_async_copy(up_hbm.at[:, at], up.at[2 * t + s], up_sem.at[2 * t + s]))
        copies.append(pair)
    downs = [
        pltpu.make_async_copy(down_hbm.at[:, pl.ds(p * wide, wide)], down.at[p], down_sem.at[p])
        for p in range(parts)
    ]
    for pair in copies:
        for c in pair:
            c.start()
    for c in downs:
        c.start()
    rows = jnp.concatenate([mine_ref[...], peer_ref[...]], axis=0)
    for t in range(tiles):
        for c in copies[t]:
            c.wait()
        weight = jnp.concatenate([up[2 * t], up[2 * t + 1]], axis=1)
        inner = jnp.dot(rows, weight, preferred_element_type=F32)
        active[:, t * 128 : (t + 1) * 128] = (silu(inner[:, :128]) * inner[:, 128:]).astype(BF16)
    for p in range(parts):
        downs[p].wait()
        result = jnp.dot(active[...], down[p], preferred_element_type=F32).astype(BF16)
        mine_out[:, p * wide : (p + 1) * wide] = result[:half]
        peer_out[:, p * wide : (p + 1) * wide] = result[half:]


def shared_kernel(count, width, *refs):
    blocks, (weights_ref, out_ref) = refs[:count], refs[count:]
    rows = blocks[0].shape[0]
    states = jnp.concatenate([b[:, :width] for b in blocks], axis=0)
    gate = jnp.dot(states, weights_ref[0], preferred_element_type=F32)
    up = jnp.dot(states, weights_ref[1], preferred_element_type=F32)
    active = (silu(gate) * up).astype(BF16)
    out_ref[...] = lax.dot_general(
        active, weights_ref[2], (((1,), (1,)), ((), ())), preferred_element_type=F32
    )


def mix_kernel(count, width, experts, capacity, me_ref, *refs):
    blocks, (mine_ref, peer_ref, shared_ref, keep_ref, leave_ref) = refs[:count], refs[count:]
    me = me_ref[0]
    peer = me_ref[1]
    rows = blocks[0].shape[0]
    for i, block in enumerate(blocks):
        match, slot = matches(block, width, experts, capacity, me, peer)
        mine, theirs = columns_of(block, width, [me, peer])
        mixing = jnp.where(match, jnp.where(slot < capacity, mine, theirs), 0.0).astype(BF16)
        at = slice(i * capacity, (i + 1) * capacity)
        results = jnp.concatenate([mine_ref[at, :], peer_ref[at, :]], axis=0)
        total = shared_ref[i * rows : (i + 1) * rows, :] + jnp.dot(
            mixing, results, preferred_element_type=F32
        )
        to = slice(i // 2 * rows, (i // 2 + 1) * rows)
        if i % 2 == 0:
            keep_ref[to, :] = total
        else:
            leave_ref[to, :] = total.astype(BF16)


def call(kernel, out_shape, in_specs, flops, nbytes, scratch=(), **kw):
    many = isinstance(out_shape, (list, tuple))
    return pl.pallas_call(
        kernel,
        out_shape=out_shape,
        in_specs=in_specs,
        out_specs=[VMEM] * len(out_shape) if many else VMEM,
        scratch_shapes=list(scratch),
        cost_estimate=pl.CostEstimate(flops=flops, bytes_accessed=nbytes, transcendentals=0),
        compiler_params=pltpu.CompilerParams(**kw),
    )


def on_device(
    hidden_state,
    norm_gain,
    router_weight,
    expert_ids,
    live_counts,
    routed_gate_up,
    routed_down,
    shared_weights,
):
    tok_rows, width = hidden_state.shape
    choose = expert_ids.shape[1]
    hidden_units = routed_down.shape[1]
    expert_count = lax.axis_size("expert")
    sub_count = lax.axis_size("sub")
    devices = expert_count * sub_count
    all_experts = routed_gate_up.shape[0] * devices
    assert routed_gate_up.shape[0] == 1 and sub_count == 2
    all_tokens = tok_rows * devices
    capacity = (tok_rows * choose * 4 + 3 * all_experts - 1) // (3 * all_experts)
    me = lax.axis_index("expert") * sub_count + lax.axis_index("sub")
    pair = jnp.stack([me, me ^ 1]).astype(jnp.int32)
    shape = jax.ShapeDtypeStruct

    def cross(block, step):
        return lax.ppermute(block, "expert", [(e, e ^ step) for e in range(expert_count)])

    def swap(block):
        return lax.ppermute(block, "sub", [(0, 1), (1, 0)])

    lanes = -(-6 * all_experts // 128) * 128
    packet = call(
        route_kernel,
        shape((tok_rows, width + lanes), BF16),
        [SMEM, VMEM, VMEM, VMEM, VMEM],
        2 * tok_rows * width * all_experts,
        4 * tok_rows * width,
    )(live_counts, hidden_state, norm_gain.reshape(1, width), router_weight, expert_ids)

    steps = expert_count // 2
    half = max(steps // 2, 1)
    chunks = [range(0, half), range(half, steps)]
    near = [cross(packet, 1)]
    direct = [packet] + [cross(packet, 2 * j) for j in range(1, steps)]
    near += [cross(direct[j], 1) for j in range(1, steps)]

    gate_up, down = routed_gate_up[0], routed_down[0]
    keeps, leaves = [None] * steps, [None] * steps
    for chunk in chunks:
        blocks = [b for j in chunk for b in (direct[j], near[j])]
        count = len(blocks)
        picked = shape((count * capacity, width), BF16)
        mine, theirs = call(
            functools.partial(pick_kernel, count, width, all_experts, capacity),
            (picked, picked),
            [SMEM] + [VMEM] * count,
            4 * count * tok_rows * capacity * width,
            8 * count * capacity * width,
        )(pair, *blocks)
        theirs = swap(theirs)
        shared = call(
            functools.partial(shared_kernel, count, width),
            shape((count * tok_rows, width), F32),
            [VMEM] * (count + 1),
            6 * count * tok_rows * width * shared_weights.shape[2],
            6 * width * shared_weights.shape[2],
        )(*blocks, shared_weights)
        parts = 4
        mine, theirs = call(
            expert_kernel,
            (picked, picked),
            [VMEM, VMEM, ANY, ANY],
            12 * count * capacity * width * hidden_units,
            6 * width * hidden_units,
            [
                pltpu.VMEM((2 * hidden_units // 128, width, 128), BF16),
                pltpu.VMEM((parts, hidden_units, width // parts), BF16),
                pltpu.VMEM((2 * count * capacity, hidden_units), BF16),
                pltpu.SemaphoreType.DMA((2 * hidden_units // 128,)),
                pltpu.SemaphoreType.DMA((parts,)),
            ],
            vmem_limit_bytes=32 << 20,
        )(mine, theirs, gate_up, down)
        theirs = swap(theirs)
        keep, leave = call(
            functools.partial(mix_kernel, count, width, all_experts, capacity),
            (shape((count // 2 * tok_rows, width), F32), shape((count // 2 * tok_rows, width), BF16)),
            [SMEM] + [VMEM] * (count + 3),
            4 * count * tok_rows * capacity * width,
            8 * count * tok_rows * width,
        )(pair, *blocks, mine, theirs, shared)
        for i, j in enumerate(chunk):
            keeps[j] = keep[i * tok_rows : (i + 1) * tok_rows]
            leaves[j] = leave[i * tok_rows : (i + 1) * tok_rows]

    mixed = None
    for j in reversed(range(steps)):
        both = keeps[j] + cross(leaves[j], 1).astype(F32)
        term = both if j == 0 else cross(both.astype(BF16), 2 * j).astype(F32)
        mixed = term if mixed is None else mixed + term
    mixed = mixed.astype(BF16)

    notes = jnp.stack([b[0, width:] for j in range(steps) for b in (direct[j], near[j])])
    notes = notes[:, 2 * all_experts : 6 * all_experts].reshape(expert_count, 4, all_experts)
    notes = jnp.stack([notes, swap(notes)]).astype(F32)
    seat = lax.axis_index("expert")
    side = lax.axis_index("sub")
    order = (jnp.arange(expert_count)[:, None] == (jnp.arange(expert_count)[None, :] ^ seat)).astype(F32)
    notes = jnp.sum(order[None, :, :, None, None] * notes[:, None], axis=2)
    load = jnp.sum(notes[:, :, 0], axis=(0, 1))
    mass = (notes[:, :, 1] + notes[:, :, 2]) + notes[:, :, 3]
    mass = jnp.sum(mass[0] + mass[1], axis=0)
    penalty = all_experts * jnp.sum(load * mass) / (choose * float(all_tokens) * float(all_tokens))
    return (mixed, penalty.reshape(1))


def solution(mesh):
    placed = (
        P(("groups", "expert", "sub"), None),
        P(),
        P(),
        P(("groups", "expert", "sub"), None),
        P(("groups", "expert", "sub")),
        P(("expert", "sub"), None, None),
        P(("expert", "sub"), None, None),
        P(None, None, "expert"),
    )
    return jax.shard_map(
        on_device,
        mesh=mesh,
        in_specs=placed,
        out_specs=(P(("groups", "expert", "sub"), None), P("groups")),
        check_vma=False,
    )
```

```python
import functools

import jax
import jax.numpy as jnp
from jax import lax
from jax.experimental import pallas as pl
from jax.experimental.pallas import tpu as pltpu
from jax.sharding import PartitionSpec as P


F32 = jnp.float32
BF16 = jnp.bfloat16
VMEM = pl.BlockSpec(memory_space=pltpu.VMEM)
SMEM = pl.BlockSpec(memory_space=pltpu.SMEM)
ANY = pl.BlockSpec(memory_space=pl.ANY)


def split_three(values):
    high = values.astype(BF16)
    rest = values - high.astype(F32)
    middle = rest.astype(BF16)
    low = (rest - middle.astype(F32)).astype(BF16)
    return high, middle, low


def iota(shape, axis):
    return lax.broadcasted_iota(jnp.int32, shape, axis)


def my_seat():
    me = lax.axis_index("expert") * 2 + lax.axis_index("sub")
    return me, me ^ 1


def route_kernel(live_ref, hidden_ref, gain_ref, router_ref, ids_ref, packet_ref):
    rows, width = hidden_ref.shape
    experts = router_ref.shape[0]
    lanes = packet_ref.shape[1] - width
    values = hidden_ref[...].astype(F32)
    spread = jnp.mean(values * values, axis=-1, keepdims=True)
    normed = (values * lax.rsqrt(spread + 1e-06) * gain_ref[...]).astype(BF16)
    packet_ref[:, :width] = normed
    logits = lax.dot_general(
        router_ref[...], normed, (((1,), (1,)), ((), ())), preferred_element_type=F32
    )
    probs = 1.0 / (1.0 + jnp.exp(-logits))
    live = (iota((1, rows), 1) < live_ref[0]).astype(F32)
    seats = iota((experts, rows), 0)
    named = jnp.zeros((experts, rows), F32)
    for k in range(ids_ref.shape[0]):
        named = named + (ids_ref[k : k + 1, :] == seats).astype(F32)
    picked = named * probs
    weights = (live * picked / jnp.sum(picked, axis=0, keepdims=True)).astype(BF16)
    taken = named * live
    earlier = (iota((rows, rows), 0) < iota((rows, rows), 1)).astype(F32).astype(BF16)
    slot = jnp.dot(taken.astype(BF16), earlier, preferred_element_type=F32)
    code = (taken * (slot + 1.0)).astype(BF16)
    load = jnp.sum(taken, axis=1, keepdims=True).astype(BF16)
    mass = jnp.sum(probs * live, axis=1, keepdims=True)
    meta = jnp.zeros((rows, lanes), F32)
    for at, piece in enumerate([weights, code, load, *split_three(mass)]):
        put = iota((experts, lanes), 1) == iota((experts, lanes), 0) + at * experts
        piece = jnp.broadcast_to(piece.astype(F32), (experts, rows)).astype(BF16)
        meta = meta + lax.dot_general(
            piece,
            put.astype(F32).astype(BF16),
            (((0,), (0,)), ((), ())),
            preferred_element_type=F32,
        )
    packet_ref[:, width:] = meta.astype(BF16)


def columns_of(block_ref, width, at):
    notes = block_ref[:, width:].astype(F32)
    lane = iota(notes.shape, 1)
    return [jnp.sum(jnp.where(lane == a, notes, 0.0), axis=1, keepdims=True) for a in at]


def matches(block_ref, width, experts, capacity):
    me, peer = my_seat()
    rows = block_ref.shape[0]
    mine, theirs = columns_of(block_ref, width, [experts + me, experts + peer])
    slot = iota((rows, 2 * capacity), 1)
    place = jnp.where(slot < capacity, mine, theirs).astype(jnp.int32)
    return (place - 1) == jnp.where(slot < capacity, slot, slot - capacity), slot


def pick_kernel(count, width, experts, capacity, *refs):
    blocks, (mine_ref, peer_ref) = refs[:count], refs[count:]
    sums = []
    for i, block in enumerate(blocks):
        match, _ = matches(block, width, experts, capacity)
        rows = lax.dot_general(
            match.astype(F32).astype(BF16),
            block[:, :width],
            (((0,), (0,)), ((), ())),
            preferred_element_type=F32,
        ).astype(BF16)
        mine_ref[i * capacity : (i + 1) * capacity, :] = rows[:capacity]
        peer_ref[i * capacity : (i + 1) * capacity, :] = rows[capacity:]
        sums.append(block[0:1, width:].astype(F32))
    filler = jnp.zeros((16 - count, sums[0].shape[1]), F32)
    sums = jnp.concatenate(sums + [filler], axis=0).astype(BF16)
    for ref in (mine_ref, peer_ref):
        ref[count * capacity :, : sums.shape[1]] = sums


def silu(value):
    return value / (1.0 + jnp.exp(-value))


def expert_kernel(mine_ref, peer_ref, up_hbm, down_hbm, mine_out, peer_out, up, down, active, up_sem, down_sem):
    half = mine_out.shape[0]
    width = mine_out.shape[1]
    units = down_hbm.shape[0]
    tiles = units // 128
    parts = down.shape[0]
    wide = width // parts
    copies = []
    for t in range(tiles):
        pair = []
        for s in range(2):
            at = pl.ds(s * units + t * 128, 128)
            pair.append(pltpu.make_async_copy(up_hbm.at[:, at], up.at[2 * t + s], up_sem.at[2 * t + s]))
        copies.append(pair)
    downs = [
        pltpu.make_async_copy(down_hbm.at[:, pl.ds(p * wide, wide)], down.at[p], down_sem.at[p])
        for p in range(parts)
    ]
    for pair in copies:
        for c in pair:
            c.start()
    for c in downs:
        c.start()
    rows = jnp.concatenate([mine_ref[:half, :], peer_ref[:half, :]], axis=0)
    for t in range(tiles):
        for c in copies[t]:
            c.wait()
        weight = jnp.concatenate([up[2 * t], up[2 * t + 1]], axis=1)
        inner = jnp.dot(rows, weight, preferred_element_type=F32)
        active[:, t * 128 : (t + 1) * 128] = (silu(inner[:, :128]) * inner[:, 128:]).astype(BF16)
    for p in range(parts):
        downs[p].wait()
        result = jnp.dot(active[...], down[p], preferred_element_type=F32).astype(BF16)
        mine_out[:, p * wide : (p + 1) * wide] = result[:half]
        peer_out[:, p * wide : (p + 1) * wide] = result[half:]


def shared_kernel(count, width, *refs):
    blocks, (weights_hbm, out_ref, weights, sems) = refs[:count], refs[count:]
    copies = [pltpu.make_async_copy(weights_hbm.at[i], weights.at[i], sems.at[i]) for i in range(3)]
    for c in copies:
        c.start()
    states = jnp.concatenate([b[:, :width] for b in blocks], axis=0)
    across = (((1,), (1,)), ((), ()))
    copies[0].wait()
    gate = lax.dot_general(states, weights[0], across, preferred_element_type=F32)
    copies[1].wait()
    up = lax.dot_general(states, weights[1], across, preferred_element_type=F32)
    active = (silu(gate) * up).astype(BF16)
    copies[2].wait()
    out_ref[...] = jnp.dot(active, weights[2], preferred_element_type=F32)


def mix_kernel(count, width, experts, capacity, *refs):
    blocks, (mine_ref, peer_ref, shared_ref), outs = refs[:count], refs[count : count + 3], refs[count + 3 :]
    me, peer = my_seat()
    rows = blocks[0].shape[0]
    for i, block in enumerate(blocks):
        match, slot = matches(block, width, experts, capacity)
        mine, theirs = columns_of(block, width, [me, peer])
        mixing = jnp.where(match, jnp.where(slot < capacity, mine, theirs), 0.0).astype(BF16)
        at = slice(i * capacity, (i + 1) * capacity)
        results = jnp.concatenate([mine_ref[at, :], peer_ref[at, :]], axis=0)
        total = shared_ref[i * rows : (i + 1) * rows, :] + jnp.dot(
            mixing, results, preferred_element_type=F32
        )
        outs[i][...] = total.astype(outs[i].dtype)


def penalty_kernel(experts, scale, *refs):
    sums, out_ref = refs[:-1], refs[-1]
    own = jnp.concatenate([s[...] for s in sums[0::2]], axis=0)
    peer = jnp.concatenate([s[...] for s in sums[1::2]], axis=0)
    seats = own.shape[0]
    seat = lax.axis_index("expert")
    order = (iota((seats, seats), 0) == (iota((seats, seats), 1) ^ seat)).astype(F32).astype(BF16)
    own = jnp.dot(order, own, preferred_element_type=F32)
    peer = jnp.dot(order, peer, preferred_element_type=F32)

    def part(array, i):
        return array[:, i * experts : (i + 1) * experts]

    load = jnp.sum(part(own, 2) + part(peer, 2), axis=0, keepdims=True)
    mass = (part(own, 3) + part(own, 4) + part(own, 5)) + (part(peer, 3) + part(peer, 4) + part(peer, 5))
    mass = jnp.sum(mass, axis=0, keepdims=True)
    out_ref[...] = jnp.sum(load * mass, axis=1, keepdims=True) * experts / scale


def call(kernel, out_shape, where, flops, nbytes, mib, scratch=()):
    spaces = {"v": pltpu.VMEM, "s": pltpu.SMEM, "h": pltpu.HBM}
    many = isinstance(out_shape, (list, tuple))
    specs = {"v": VMEM, "s": SMEM, "h": pl.BlockSpec(memory_space=pltpu.HBM)}

    def vmem(x):
        return pltpu.VMEM(x.shape, x.dtype)

    run = pl.pallas_call(
        kernel,
        out_shape=[vmem(x) for x in out_shape] if many else vmem(out_shape),
        in_specs=[specs[w] for w in where],
        out_specs=[VMEM] * len(out_shape) if many else VMEM,
        scratch_shapes=list(scratch),
        cost_estimate=pl.CostEstimate(flops=flops, bytes_accessed=nbytes, transcendentals=0),
        compiler_params=pltpu.CompilerParams(vmem_limit_bytes=mib << 20),
    )

    def go(*args):
        args = [
            a if w == "s" else pltpu.with_memory_space_constraint(a, spaces[w])
            for a, w in zip(args, where)
        ]
        return run(*args)

    return go


def chunks_of(steps):
    half = max(steps // 2, 1)
    return [range(0, half), range(half, steps)]


def on_device(
    hidden_state,
    norm_gain,
    router_weight,
    expert_ids,
    live_counts,
    routed_gate_up,
    routed_down,
    shared_weights,
):
    tok_rows, width = hidden_state.shape
    choose = expert_ids.shape[1]
    hidden_units = routed_down.shape[1]
    expert_count = lax.axis_size("expert")
    sub_count = lax.axis_size("sub")
    devices = expert_count * sub_count
    all_experts = routed_gate_up.shape[0] * devices
    assert routed_gate_up.shape[0] == 1 and sub_count == 2
    all_tokens = tok_rows * devices
    capacity = (tok_rows * choose * 4 + 3 * all_experts - 1) // (3 * all_experts)
    shape = jax.ShapeDtypeStruct

    def cross(block, step):
        return lax.ppermute(block, "expert", [(e, e ^ step) for e in range(expert_count)])

    def swap(block):
        return lax.ppermute(block, "sub", [(0, 1), (1, 0)])

    lanes = -(-6 * all_experts // 128) * 128
    packet = call(
        route_kernel,
        shape((tok_rows, width + lanes), BF16),
        "svvvv",
        2 * tok_rows * width * all_experts,
        4 * tok_rows * width,
        8,
    )(live_counts, hidden_state, norm_gain.reshape(1, width), router_weight.T, expert_ids.T)

    steps = expert_count // 2
    chunks = chunks_of(steps)
    direct = [packet] + [cross(packet, 2 * j) for j in range(1, steps)]
    near = [cross(direct[j], 1) for j in range(steps)]

    gate_up, down = routed_gate_up[0], routed_down[0]
    shared_rows = jnp.swapaxes(shared_weights, 1, 2)
    keeps, leaves, sums = [None] * steps, [None] * steps, []
    for chunk in chunks:
        blocks = [b for j in chunk for b in (direct[j], near[j])]
        count = len(blocks)
        picked = shape((count * capacity + 16, width), BF16)
        results = shape((count * capacity, width), BF16)
        mine, theirs = call(
            functools.partial(pick_kernel, count, width, all_experts, capacity),
            (picked, picked),
            "v" * count,
            4 * count * tok_rows * capacity * width,
            8 * count * capacity * width,
            12,
        )(*blocks)
        theirs = swap(theirs)
        shared = call(
            functools.partial(shared_kernel, count, width),
            shape((count * tok_rows, width), F32),
            "v" * count + "h",
            6 * count * tok_rows * width * shared_rows.shape[1],
            6 * width * shared_rows.shape[1],
            24,
            [pltpu.VMEM(shared_rows.shape, BF16), pltpu.SemaphoreType.DMA((3,))],
        )(*blocks, shared_rows)
        sums += [x[count * capacity :][:count, :lanes] for x in (mine, theirs)]
        parts = 4
        mine, theirs = call(
            expert_kernel,
            (results, results),
            "vvhh",
            12 * count * capacity * width * hidden_units,
            6 * width * hidden_units,
            32,
            [
                pltpu.VMEM((2 * hidden_units // 128, width, 128), BF16),
                pltpu.VMEM((parts, hidden_units, width // parts), BF16),
                pltpu.VMEM((2 * count * capacity, hidden_units), BF16),
                pltpu.SemaphoreType.DMA((2 * hidden_units // 128,)),
                pltpu.SemaphoreType.DMA((parts,)),
            ],
        )(mine, theirs, gate_up, down)
        theirs = swap(theirs)
        tokens = (tok_rows, width)
        totals = call(
            functools.partial(mix_kernel, count, width, all_experts, capacity),
            [shape(tokens, F32), shape(tokens, BF16)] * (count // 2),
            "v" * (count + 3),
            4 * count * tok_rows * capacity * width,
            8 * count * tok_rows * width,
            16,
        )(*blocks, mine, theirs, shared)
        for i, j in enumerate(chunk):
            keeps[j], leaves[j] = totals[2 * i], totals[2 * i + 1]

    mixed = None
    for j in reversed(range(steps)):
        both = keeps[j] + cross(leaves[j], 1).astype(F32)
        term = both if j == 0 else cross(both.astype(BF16), 2 * j).astype(F32)
        mixed = term if mixed is None else mixed + term
    mixed = mixed.astype(BF16)

    penalty = call(
        functools.partial(penalty_kernel, all_experts, choose * float(all_tokens) * float(all_tokens)),
        shape((1, 1), F32),
        "v" * len(sums),
        0,
        0,
        4,
    )(*sums)
    return (mixed, penalty.reshape(1))


def solution(mesh):
    placed = (
        P(("groups", "expert", "sub"), None),
        P(),
        P(),
        P(("groups", "expert", "sub"), None),
        P(("groups", "expert", "sub")),
        P(("expert", "sub"), None, None),
        P(("expert", "sub"), None, None),
        P(None, None, "expert"),
    )

    return jax.shard_map(
        on_device,
        mesh=mesh,
        in_specs=placed,
        out_specs=(P(("groups", "expert", "sub"), None), P("groups")),
        check_vma=False,
    )
```

```python
import functools

import jax
import jax.numpy as jnp
from jax import lax
from jax.experimental import pallas as pl
from jax.experimental.pallas import tpu as pltpu
from jax.sharding import PartitionSpec as P


F32 = jnp.float32
BF16 = jnp.bfloat16
VMEM = pl.BlockSpec(memory_space=pltpu.VMEM)
SMEM = pl.BlockSpec(memory_space=pltpu.SMEM)
ANY = pl.BlockSpec(memory_space=pl.ANY)


def split_three(values):
    high = values.astype(BF16)
    rest = values - high.astype(F32)
    middle = rest.astype(BF16)
    low = (rest - middle.astype(F32)).astype(BF16)
    return high, middle, low


def iota(shape, axis):
    return lax.broadcasted_iota(jnp.int32, shape, axis)


def my_seat():
    me = lax.axis_index("expert") * 2 + lax.axis_index("sub")
    return me, me ^ 1


def route_kernel(live_ref, hidden_hbm, gain_hbm, router_hbm, ids_hbm, packet_ref, hidden_ref, gain_ref, router_ref, ids_ref, sems):
    pairs = ((hidden_hbm, hidden_ref), (gain_hbm, gain_ref), (router_hbm, router_ref), (ids_hbm, ids_ref))
    copies = [pltpu.make_async_copy(x, y, sems.at[i]) for i, (x, y) in enumerate(pairs)]
    for c in copies:
        c.start()
    for c in copies:
        c.wait()
    rows, width = hidden_ref.shape
    experts = router_ref.shape[0]
    lanes = packet_ref.shape[1] - width
    values = hidden_ref[...].astype(F32)
    spread = jnp.mean(values * values, axis=-1, keepdims=True)
    normed = (values * lax.rsqrt(spread + 1e-06) * gain_ref[...]).astype(BF16)
    packet_ref[:, :width] = normed
    logits = lax.dot_general(
        router_ref[...], normed, (((1,), (1,)), ((), ())), preferred_element_type=F32
    )
    probs = 1.0 / (1.0 + jnp.exp(-logits))
    live = (iota((1, rows), 1) < live_ref[0]).astype(F32)
    seats = iota((experts, rows), 0)
    named = jnp.zeros((experts, rows), F32)
    for k in range(ids_ref.shape[0]):
        named = named + (ids_ref[k : k + 1, :] == seats).astype(F32)
    picked = named * probs
    weights = (live * picked / jnp.sum(picked, axis=0, keepdims=True)).astype(BF16)
    taken = named * live
    earlier = (iota((rows, rows), 0) < iota((rows, rows), 1)).astype(F32).astype(BF16)
    slot = jnp.dot(taken.astype(BF16), earlier, preferred_element_type=F32)
    code = (taken * (slot + 1.0)).astype(BF16)
    load = jnp.sum(taken, axis=1, keepdims=True).astype(BF16)
    mass = jnp.sum(probs * live, axis=1, keepdims=True)
    meta = jnp.zeros((rows, lanes), F32)
    for at, piece in enumerate([weights, code, load, *split_three(mass)]):
        put = iota((experts, lanes), 1) == iota((experts, lanes), 0) + at * experts
        piece = jnp.broadcast_to(piece.astype(F32), (experts, rows)).astype(BF16)
        meta = meta + lax.dot_general(
            piece,
            put.astype(F32).astype(BF16),
            (((0,), (0,)), ((), ())),
            preferred_element_type=F32,
        )
    packet_ref[:, width:] = meta.astype(BF16)


def columns_of(block_ref, width, at):
    notes = block_ref[:, width:].astype(F32)
    lane = iota(notes.shape, 1)
    return [jnp.sum(jnp.where(lane == a, notes, 0.0), axis=1, keepdims=True) for a in at]


def matches(block_ref, width, experts, capacity):
    me, peer = my_seat()
    rows = block_ref.shape[0]
    mine, theirs = columns_of(block_ref, width, [experts + me, experts + peer])
    slot = iota((rows, 2 * capacity), 1)
    place = jnp.where(slot < capacity, mine, theirs).astype(jnp.int32)
    return (place - 1) == jnp.where(slot < capacity, slot, slot - capacity), slot


def pick_kernel(count, width, experts, capacity, *refs):
    blocks, (mine_ref, peer_ref) = refs[:count], refs[count:]
    sums = []
    for i, block in enumerate(blocks):
        match, _ = matches(block, width, experts, capacity)
        rows = lax.dot_general(
            match.astype(F32).astype(BF16),
            block[:, :width],
            (((0,), (0,)), ((), ())),
            preferred_element_type=F32,
        ).astype(BF16)
        mine_ref[i * capacity : (i + 1) * capacity, :] = rows[:capacity]
        peer_ref[i * capacity : (i + 1) * capacity, :] = rows[capacity:]
        sums.append(block[0:1, width:].astype(F32))
    filler = jnp.zeros((16 - count, sums[0].shape[1]), F32)
    sums = jnp.concatenate(sums + [filler], axis=0).astype(BF16)
    for ref in (mine_ref, peer_ref):
        ref[count * capacity :, : sums.shape[1]] = sums


def silu(value):
    return value / (1.0 + jnp.exp(-value))


def load_kernel(*refs):
    count = (len(refs) - 1) // 2
    sems = refs[-1]
    copies = [pltpu.make_async_copy(refs[i], refs[count + i], sems.at[i]) for i in range(count)]
    for c in copies:
        c.start()
    for c in copies:
        c.wait()


def expert_kernel(mine_ref, peer_ref, up_ref, down_ref, mine_out, peer_out, active):
    half, width = mine_out.shape
    units = down_ref.shape[0]
    rows = jnp.concatenate([mine_ref[:half, :], peer_ref[:half, :]], axis=0)
    for at in range(0, units, 256):
        to = min(at + 256, units)
        gate = jnp.dot(rows, up_ref[:, at:to], preferred_element_type=F32)
        up = jnp.dot(rows, up_ref[:, units + at : units + to], preferred_element_type=F32)
        active[:, at:to] = (silu(gate) * up).astype(BF16)
    for at in range(0, width, 512):
        to = min(at + 512, width)
        result = jnp.dot(active[...], down_ref[:, at:to], preferred_element_type=F32).astype(BF16)
        mine_out[:, at:to] = result[:half]
        peer_out[:, at:to] = result[half:]


def shared_kernel(count, width, *refs):
    blocks, (weights_ref, out_ref) = refs[:count], refs[count:]
    states = jnp.concatenate([b[:, :width] for b in blocks], axis=0)
    across = (((1,), (1,)), ((), ()))
    gate = lax.dot_general(states, weights_ref[0], across, preferred_element_type=F32)
    up = lax.dot_general(states, weights_ref[1], across, preferred_element_type=F32)
    active = (silu(gate) * up).astype(BF16)
    out_ref[...] = jnp.dot(active, weights_ref[2], preferred_element_type=F32)


def mix_kernel(count, width, experts, capacity, *refs):
    blocks, (mine_ref, peer_ref, shared_ref), outs = refs[:count], refs[count : count + 3], refs[count + 3 :]
    me, peer = my_seat()
    rows = blocks[0].shape[0]
    for i, block in enumerate(blocks):
        match, slot = matches(block, width, experts, capacity)
        mine, theirs = columns_of(block, width, [me, peer])
        mixing = jnp.where(match, jnp.where(slot < capacity, mine, theirs), 0.0).astype(BF16)
        at = slice(i * capacity, (i + 1) * capacity)
        results = jnp.concatenate([mine_ref[at, :], peer_ref[at, :]], axis=0)
        total = shared_ref[i * rows : (i + 1) * rows, :] + jnp.dot(
            mixing, results, preferred_element_type=F32
        )
        outs[i][...] = total.astype(outs[i].dtype)


def penalty_kernel(experts, scale, steps, *refs):
    sums, out_ref = refs[:-1], refs[-1]
    own = jnp.concatenate([s[...] for s in sums[0::2]], axis=0)
    peer = jnp.concatenate([s[...] for s in sums[1::2]], axis=0)
    seats = own.shape[0]
    seat = lax.axis_index("expert")
    row = iota((seats, seats), 1)
    step = jnp.zeros_like(row)
    for r, k in enumerate(steps):
        step = jnp.where(row == r, k, step)
    order = (iota((seats, seats), 0) == (step ^ seat)).astype(F32).astype(BF16)
    own = jnp.dot(order, own, preferred_element_type=F32)
    peer = jnp.dot(order, peer, preferred_element_type=F32)

    def part(array, i):
        return array[:, i * experts : (i + 1) * experts]

    load = jnp.sum(part(own, 2) + part(peer, 2), axis=0, keepdims=True)
    mass = (part(own, 3) + part(own, 4) + part(own, 5)) + (part(peer, 3) + part(peer, 4) + part(peer, 5))
    mass = jnp.sum(mass, axis=0, keepdims=True)
    out_ref[...] = jnp.sum(load * mass, axis=1, keepdims=True) * experts / scale


def call(kernel, out_shape, where, flops, nbytes, mib, scratch=()):
    spaces = {"v": pltpu.VMEM, "s": pltpu.SMEM, "h": pltpu.HBM}
    many = isinstance(out_shape, (list, tuple))
    specs = {"v": VMEM, "s": SMEM, "h": pl.BlockSpec(memory_space=pltpu.HBM)}

    def vmem(x):
        return pltpu.VMEM(x.shape, x.dtype)

    run = pl.pallas_call(
        kernel,
        out_shape=[vmem(x) for x in out_shape] if many else vmem(out_shape),
        in_specs=[specs[w] for w in where],
        out_specs=[VMEM] * len(out_shape) if many else VMEM,
        scratch_shapes=list(scratch),
        cost_estimate=pl.CostEstimate(flops=flops, bytes_accessed=nbytes, transcendentals=0),
        compiler_params=pltpu.CompilerParams(vmem_limit_bytes=mib << 20),
    )

    def go(*args):
        args = [
            a if w == "s" else pltpu.with_memory_space_constraint(a, spaces[w])
            for a, w in zip(args, where)
        ]
        return run(*args)

    return go


def chunks_of(steps):
    return [list(range(0, steps, 2)), list(range(1, steps, 2))]


def on_device(
    hidden_state,
    norm_gain,
    router_weight,
    expert_ids,
    live_counts,
    routed_gate_up,
    routed_down,
    shared_weights,
):
    tok_rows, width = hidden_state.shape
    choose = expert_ids.shape[1]
    hidden_units = routed_down.shape[1]
    expert_count = lax.axis_size("expert")
    sub_count = lax.axis_size("sub")
    devices = expert_count * sub_count
    all_experts = routed_gate_up.shape[0] * devices
    assert routed_gate_up.shape[0] == 1 and sub_count == 2
    all_tokens = tok_rows * devices
    capacity = (tok_rows * choose * 4 + 3 * all_experts - 1) // (3 * all_experts)
    shape = jax.ShapeDtypeStruct

    def cross(block, step):
        return lax.ppermute(block, "expert", [(e, e ^ step) for e in range(expert_count)])

    def swap(block):
        return lax.ppermute(block, "sub", [(0, 1), (1, 0)])

    lanes = -(-6 * all_experts // 128) * 128
    packet = call(
        route_kernel,
        shape((tok_rows, width + lanes), BF16),
        "shhhh",
        2 * tok_rows * width * all_experts,
        4 * tok_rows * width,
        8,
        [
            pltpu.VMEM((tok_rows, width), BF16),
            pltpu.VMEM((1, width), F32),
            pltpu.VMEM((all_experts, width), BF16),
            pltpu.VMEM((choose, tok_rows), jnp.int32),
            pltpu.SemaphoreType.DMA((4,)),
        ],
    )(live_counts, hidden_state, norm_gain.reshape(1, width), router_weight.T, expert_ids.T)

    steps = expert_count // 2
    chunks = chunks_of(steps)
    direct = [packet] + [cross(packet, 2 * j) for j in range(1, steps)]
    near = [cross(direct[j], 1) for j in range(steps)]

    def load(*arrays):
        return call(
            load_kernel,
            [shape(a.shape, a.dtype) for a in arrays],
            "h" * len(arrays),
            0,
            sum(2 * a.size for a in arrays),
            1,
            [pltpu.SemaphoreType.DMA((len(arrays),))],
        )(*arrays)

    (gate_up,) = load(routed_gate_up[0])
    down, shared_rows = load(routed_down[0], jnp.swapaxes(shared_weights, 1, 2))
    keeps, leaves, sums = [None] * steps, [None] * steps, []
    for chunk in chunks:
        blocks = [b for j in chunk for b in (direct[j], near[j])]
        count = len(blocks)
        picked = shape((count * capacity + 16, width), BF16)
        results = shape((count * capacity, width), BF16)
        mine, theirs = call(
            functools.partial(pick_kernel, count, width, all_experts, capacity),
            (picked, picked),
            "v" * count,
            4 * count * tok_rows * capacity * width,
            8 * count * capacity * width,
            8,
        )(*blocks)
        theirs = swap(theirs)
        shared = call(
            functools.partial(shared_kernel, count, width),
            shape((count * tok_rows, width), F32),
            "v" * (count + 1),
            6 * count * tok_rows * width * shared_rows.shape[1],
            6 * width * shared_rows.shape[1],
            8,
        )(*blocks, shared_rows)
        sums += [x[count * capacity :][:count, :lanes] for x in (mine, theirs)]
        mine, theirs = call(
            expert_kernel,
            (results, results),
            "vvvv",
            12 * count * capacity * width * hidden_units,
            6 * width * hidden_units,
            8,
            [pltpu.VMEM((2 * count * capacity, hidden_units), BF16)],
        )(mine, theirs, gate_up, down)
        theirs = swap(theirs)
        tokens = (tok_rows, width)
        totals = call(
            functools.partial(mix_kernel, count, width, all_experts, capacity),
            [shape(tokens, F32), shape(tokens, BF16)] * (count // 2),
            "v" * (count + 3),
            4 * count * tok_rows * capacity * width,
            8 * count * tok_rows * width,
            8,
        )(*blocks, mine, theirs, shared)
        for i, j in enumerate(chunk):
            keeps[j], leaves[j] = totals[2 * i], totals[2 * i + 1]

    mixed = None
    for j in reversed(range(steps)):
        both = keeps[j] + cross(leaves[j], 1).astype(F32)
        term = both if j == 0 else cross(both.astype(BF16), 2 * j).astype(F32)
        mixed = term if mixed is None else mixed + term
    mixed = mixed.astype(BF16)

    penalty = call(
        functools.partial(
            penalty_kernel,
            all_experts,
            choose * float(all_tokens) * float(all_tokens),
            [2 * j + b for chunk in chunks for j in chunk for b in range(2)],
        ),
        shape((1, 1), F32),
        "v" * len(sums),
        0,
        0,
        4,
    )(*sums)
    return (mixed, penalty.reshape(1))


def solution(mesh):
    placed = (
        P(("groups", "expert", "sub"), None),
        P(),
        P(),
        P(("groups", "expert", "sub"), None),
        P(("groups", "expert", "sub")),
        P(("expert", "sub"), None, None),
        P(("expert", "sub"), None, None),
        P(None, None, "expert"),
    )

    return jax.shard_map(
        on_device,
        mesh=mesh,
        in_specs=placed,
        out_specs=(P(("groups", "expert", "sub"), None), P("groups")),
        check_vma=False,
    )
```

```python
import functools

import jax
import jax.numpy as jnp
from jax import lax
from jax.experimental import pallas as pl
from jax.experimental.pallas import tpu as pltpu
from jax.sharding import PartitionSpec as P


F32 = jnp.float32
BF16 = jnp.bfloat16
VMEM = pl.BlockSpec(memory_space=pltpu.VMEM)
SMEM = pl.BlockSpec(memory_space=pltpu.SMEM)
ANY = pl.BlockSpec(memory_space=pl.ANY)


def split_three(values):
    high = values.astype(BF16)
    rest = values - high.astype(F32)
    middle = rest.astype(BF16)
    low = (rest - middle.astype(F32)).astype(BF16)
    return high, middle, low


def iota(shape, axis):
    return lax.broadcasted_iota(jnp.int32, shape, axis)


def my_seat():
    me = lax.axis_index("expert") * 2 + lax.axis_index("sub")
    return me, me ^ 1


def route_kernel(
    live_ref, hidden_hbm, gain_hbm, router_hbm, ids_hbm, packet_ref, hidden_ref, gain_ref, router_ref, ids_ref, sems
):
    pairs = (
        (hidden_hbm, hidden_ref),
        (gain_hbm, gain_ref),
        (router_hbm, router_ref),
        (ids_hbm, ids_ref),
    )
    copies = [pltpu.make_async_copy(x, y, sems.at[i]) for i, (x, y) in enumerate(pairs)]
    for c in copies:
        c.start()
    for c in copies:
        c.wait()
    rows, width = hidden_ref.shape
    experts = router_ref.shape[0]
    lanes = packet_ref.shape[1] - width
    values = hidden_ref[...].astype(F32)
    spread = jnp.mean(values * values, axis=-1, keepdims=True)
    normed = (values * lax.rsqrt(spread + 1e-06) * gain_ref[...]).astype(BF16)
    packet_ref[:, :width] = normed
    logits = lax.dot_general(
        router_ref[...], normed, (((1,), (1,)), ((), ())), preferred_element_type=F32
    )
    probs = 1.0 / (1.0 + jnp.exp(-logits))
    live = (iota((1, rows), 1) < live_ref[0]).astype(F32)
    seats = iota((experts, rows), 0)
    named = jnp.zeros((experts, rows), F32)
    for k in range(ids_ref.shape[0]):
        named = named + (ids_ref[k : k + 1, :] == seats).astype(F32)
    picked = named * probs
    weights = (live * picked / jnp.sum(picked, axis=0, keepdims=True)).astype(BF16)
    taken = named * live
    earlier = (iota((rows, rows), 0) < iota((rows, rows), 1)).astype(F32).astype(BF16)
    slot = jnp.dot(taken.astype(BF16), earlier, preferred_element_type=F32)
    code = (taken * (slot + 1.0)).astype(BF16)
    load = jnp.sum(taken, axis=1, keepdims=True).astype(BF16)
    mass = jnp.sum(probs * live, axis=1, keepdims=True)
    meta = jnp.zeros((rows, lanes), F32)
    for at, piece in enumerate([weights, code, load, *split_three(mass)]):
        put = iota((experts, lanes), 1) == iota((experts, lanes), 0) + at * experts
        piece = jnp.broadcast_to(piece.astype(F32), (experts, rows)).astype(BF16)
        meta = meta + lax.dot_general(
            piece,
            put.astype(F32).astype(BF16),
            (((0,), (0,)), ((), ())),
            preferred_element_type=F32,
        )
    packet_ref[:, width:] = meta.astype(BF16)


def columns_of(block_ref, width, at):
    notes = block_ref[:, width:].astype(F32)
    lane = iota(notes.shape, 1)
    return [jnp.sum(jnp.where(lane == a, notes, 0.0), axis=1, keepdims=True) for a in at]


def matches(block_ref, width, experts, capacity):
    me, peer = my_seat()
    rows = block_ref.shape[0]
    mine, theirs = columns_of(block_ref, width, [experts + me, experts + peer])
    slot = iota((rows, 2 * capacity), 1)
    place = jnp.where(slot < capacity, mine, theirs).astype(jnp.int32)
    return (place - 1) == jnp.where(slot < capacity, slot, slot - capacity), slot


def pick_kernel(count, width, experts, capacity, *refs):
    blocks, (mine_ref, peer_ref) = refs[:count], refs[count:]
    sums = []
    for i, block in enumerate(blocks):
        match, _ = matches(block, width, experts, capacity)
        rows = lax.dot_general(
            match.astype(F32).astype(BF16),
            block[:, :width],
            (((0,), (0,)), ((), ())),
            preferred_element_type=F32,
        ).astype(BF16)
        mine_ref[i * capacity : (i + 1) * capacity, :] = rows[:capacity]
        peer_ref[i * capacity : (i + 1) * capacity, :] = rows[capacity:]
        sums.append(block[0:1, width:].astype(F32))
    filler = jnp.zeros((16 - count, sums[0].shape[1]), F32)
    sums = jnp.concatenate(sums + [filler], axis=0).astype(BF16)
    for ref in (mine_ref, peer_ref):
        ref[count * capacity :, : sums.shape[1]] = sums


def silu(value):
    return value / (1.0 + jnp.exp(-value))


def load_kernel(*refs):
    count = (len(refs) - 1) // 2
    sems = refs[-1]
    copies = [pltpu.make_async_copy(refs[i], refs[count + i], sems.at[i]) for i in range(count)]
    for c in copies:
        c.start()
    for c in copies:
        c.wait()


def expert_kernel(mine_ref, peer_ref, up_ref, down_ref, mine_out, peer_out, active):
    half, width = mine_out.shape
    units = down_ref.shape[0]
    rows = jnp.concatenate([mine_ref[:half, :], peer_ref[:half, :]], axis=0)
    for at in range(0, units, 256):
        to = min(at + 256, units)
        gate = jnp.dot(rows, up_ref[:, at:to], preferred_element_type=F32)
        up = jnp.dot(rows, up_ref[:, units + at : units + to], preferred_element_type=F32)
        active[:, at:to] = (silu(gate) * up).astype(BF16)
    for at in range(0, width, 512):
        to = min(at + 512, width)
        result = jnp.dot(active[...], down_ref[:, at:to], preferred_element_type=F32).astype(BF16)
        mine_out[:, at:to] = result[:half]
        peer_out[:, at:to] = result[half:]


def shared_kernel(count, width, *refs):
    blocks, (weights_ref, out_ref) = refs[:count], refs[count:]
    states = jnp.concatenate([b[:, :width] for b in blocks], axis=0)
    across = (((1,), (1,)), ((), ()))
    gate = lax.dot_general(states, weights_ref[0], across, preferred_element_type=F32)
    up = lax.dot_general(states, weights_ref[1], across, preferred_element_type=F32)
    active = (silu(gate) * up).astype(BF16)
    out_ref[...] = jnp.dot(active, weights_ref[2], preferred_element_type=F32)


def mix_kernel(count, width, experts, capacity, *refs):
    blocks, (mine_ref, peer_ref, shared_ref), outs = refs[:count], refs[count : count + 3], refs[count + 3 :]
    me, peer = my_seat()
    rows = blocks[0].shape[0]
    for i, block in enumerate(blocks):
        match, slot = matches(block, width, experts, capacity)
        mine, theirs = columns_of(block, width, [me, peer])
        mixing = jnp.where(match, jnp.where(slot < capacity, mine, theirs), 0.0).astype(BF16)
        at = slice(i * capacity, (i + 1) * capacity)
        results = jnp.concatenate([mine_ref[at, :], peer_ref[at, :]], axis=0)
        total = shared_ref[i * rows : (i + 1) * rows, :] + jnp.dot(
            mixing, results, preferred_element_type=F32
        )
        outs[i][...] = total.astype(outs[i].dtype)


def penalty_kernel(experts, scale, steps, *refs):
    sums, out_ref = refs[:-1], refs[-1]
    own = jnp.concatenate([s[...] for s in sums[0::2]], axis=0)
    peer = jnp.concatenate([s[...] for s in sums[1::2]], axis=0)
    seats = own.shape[0]
    seat = lax.axis_index("expert")
    row = iota((seats, seats), 1)
    step = jnp.zeros_like(row)
    for r, k in enumerate(steps):
        step = jnp.where(row == r, k, step)
    order = (iota((seats, seats), 0) == (step ^ seat)).astype(F32).astype(BF16)
    own = jnp.dot(order, own, preferred_element_type=F32)
    peer = jnp.dot(order, peer, preferred_element_type=F32)

    def part(array, i):
        return array[:, i * experts : (i + 1) * experts]

    load = jnp.sum(part(own, 2) + part(peer, 2), axis=0, keepdims=True)
    mass = (part(own, 3) + part(own, 4) + part(own, 5)) + (part(peer, 3) + part(peer, 4) + part(peer, 5))
    mass = jnp.sum(mass, axis=0, keepdims=True)
    out_ref[...] = jnp.sum(load * mass, axis=1, keepdims=True) * experts / scale


def call(kernel, out_shape, where, flops, nbytes, mib, scratch=()):
    spaces = {"v": pltpu.VMEM, "s": pltpu.SMEM, "h": pltpu.HBM}
    many = isinstance(out_shape, (list, tuple))
    specs = {"v": VMEM, "s": SMEM, "h": pl.BlockSpec(memory_space=pltpu.HBM)}

    def vmem(x):
        return pltpu.VMEM(x.shape, x.dtype)

    run = pl.pallas_call(
        kernel,
        out_shape=[vmem(x) for x in out_shape] if many else vmem(out_shape),
        in_specs=[specs[w] for w in where],
        out_specs=[VMEM] * len(out_shape) if many else VMEM,
        scratch_shapes=list(scratch),
        cost_estimate=pl.CostEstimate(flops=flops, bytes_accessed=nbytes, transcendentals=0),
        compiler_params=pltpu.CompilerParams(vmem_limit_bytes=mib << 20),
    )

    def go(*args):
        args = [
            a if w == "s" else pltpu.with_memory_space_constraint(a, spaces[w])
            for a, w in zip(args, where)
        ]
        return run(*args)

    return go


def chunks_of(steps):
    return [list(range(0, steps, 2)), list(range(1, steps, 2))]


def on_device(
    hidden_state,
    norm_gain,
    router_weight,
    expert_ids,
    live_counts,
    routed_gate_up,
    routed_down,
    shared_weights,
):
    tok_rows, width = hidden_state.shape
    choose = expert_ids.shape[1]
    hidden_units = routed_down.shape[1]
    expert_count = lax.axis_size("expert")
    sub_count = lax.axis_size("sub")
    devices = expert_count * sub_count
    all_experts = routed_gate_up.shape[0] * devices
    assert routed_gate_up.shape[0] == 1 and sub_count == 2
    all_tokens = tok_rows * devices
    capacity = (tok_rows * choose * 4 + 3 * all_experts - 1) // (3 * all_experts)
    shape = jax.ShapeDtypeStruct

    def cross(block, step):
        return lax.ppermute(block, "expert", [(e, e ^ step) for e in range(expert_count)])

    def swap(block):
        return lax.ppermute(block, "sub", [(0, 1), (1, 0)])

    lanes = -(-6 * all_experts // 128) * 128
    packet = call(
        route_kernel,
        shape((tok_rows, width + lanes), BF16),
        "shhhh",
        2 * tok_rows * width * all_experts,
        4 * tok_rows * width,
        8,
        [
            pltpu.VMEM((tok_rows, width), BF16),
            pltpu.VMEM((1, width), F32),
            pltpu.VMEM((all_experts, width), BF16),
            pltpu.VMEM((choose, tok_rows), jnp.int32),
            pltpu.SemaphoreType.DMA((4,)),
        ],
    )(live_counts, hidden_state, norm_gain.reshape(1, width), router_weight.T, expert_ids.T)

    steps = expert_count // 2
    chunks = chunks_of(steps)
    direct = [packet, cross(packet, 2)]
    for j in range(2, steps):
        direct.append(cross(direct[j - 1], 2) if j % 2 else cross(packet, 2 * j))
    near = [cross(direct[j], 1) for j in range(steps)]

    def load(*arrays):
        return call(
            load_kernel,
            [shape(a.shape, a.dtype) for a in arrays],
            "h" * len(arrays),
            0,
            sum(2 * a.size for a in arrays),
            1,
            [pltpu.SemaphoreType.DMA((len(arrays),))],
        )(*arrays)

    (gate_up,) = load(routed_gate_up[0])
    down, shared_rows = load(routed_down[0], jnp.swapaxes(shared_weights, 1, 2))
    keeps, leaves, sums = [None] * steps, [None] * steps, []
    for chunk in chunks:
        blocks = [b for j in chunk for b in (direct[j], near[j])]
        count = len(blocks)
        picked = shape((count * capacity + 16, width), BF16)
        results = shape((count * capacity, width), BF16)
        mine, theirs = call(
            functools.partial(pick_kernel, count, width, all_experts, capacity),
            (picked, picked),
            "v" * count,
            4 * count * tok_rows * capacity * width,
            8 * count * capacity * width,
            8,
        )(*blocks)
        theirs = swap(theirs)
        shared = call(
            functools.partial(shared_kernel, count, width),
            shape((count * tok_rows, width), F32),
            "v" * (count + 1),
            6 * count * tok_rows * width * shared_rows.shape[1],
            6 * width * shared_rows.shape[1],
            8,
        )(*blocks, shared_rows)
        sums += [x[count * capacity :][:count, :lanes] for x in (mine, theirs)]
        mine, theirs = call(
            expert_kernel,
            (results, results),
            "vvvv",
            12 * count * capacity * width * hidden_units,
            6 * width * hidden_units,
            8,
            [pltpu.VMEM((2 * count * capacity, hidden_units), BF16)],
        )(mine, theirs, gate_up, down)
        theirs = swap(theirs)
        tokens = (tok_rows, width)
        totals = call(
            functools.partial(mix_kernel, count, width, all_experts, capacity),
            [shape(tokens, F32), shape(tokens, BF16)] * (count // 2),
            "v" * (count + 3),
            4 * count * tok_rows * capacity * width,
            8 * count * tok_rows * width,
            8,
        )(*blocks, mine, theirs, shared)
        for i, j in enumerate(chunk):
            keeps[j], leaves[j] = totals[2 * i], totals[2 * i + 1]

    mixed = None
    for j in reversed(range(steps)):
        both = keeps[j] + cross(leaves[j], 1).astype(F32)
        term = both if j == 0 else cross(both.astype(BF16), 2 * j).astype(F32)
        mixed = term if mixed is None else mixed + term
    mixed = mixed.astype(BF16)

    penalty = call(
        functools.partial(
            penalty_kernel,
            all_experts,
            choose * float(all_tokens) * float(all_tokens),
            [2 * j + b for chunk in chunks for j in chunk for b in range(2)],
        ),
        shape((1, 1), F32),
        "v" * len(sums),
        0,
        0,
        4,
    )(*sums)
    return (mixed, penalty.reshape(1))


def solution(mesh):
    placed = (
        P(("groups", "expert", "sub"), None),
        P(),
        P(),
        P(("groups", "expert", "sub"), None),
        P(("groups", "expert", "sub")),
        P(("expert", "sub"), None, None),
        P(("expert", "sub"), None, None),
        P(None, None, "expert"),
    )

    return jax.shard_map(
        on_device,
        mesh=mesh,
        in_specs=placed,
        out_specs=(P(("groups", "expert", "sub"), None), P("groups")),
        check_vma=False,
    )
```

```python
import functools

import jax
import jax.numpy as jnp
from jax import lax
from jax.experimental import pallas as pl
from jax.experimental.pallas import tpu as pltpu
from jax.sharding import PartitionSpec as P


F32 = jnp.float32
BF16 = jnp.bfloat16
VMEM = pl.BlockSpec(memory_space=pltpu.VMEM)
SMEM = pl.BlockSpec(memory_space=pltpu.SMEM)
ANY = pl.BlockSpec(memory_space=pl.ANY)


def split_three(values):
    high = values.astype(BF16)
    rest = values - high.astype(F32)
    middle = rest.astype(BF16)
    low = (rest - middle.astype(F32)).astype(BF16)
    return high, middle, low


def iota(shape, axis):
    return lax.broadcasted_iota(jnp.int32, shape, axis)


def my_seat():
    me = lax.axis_index("expert") * 2 + lax.axis_index("sub")
    return me, me ^ 1


def route_kernel(
    live_ref, hidden_hbm, gain_hbm, router_hbm, ids_hbm, packet_ref, hidden_ref, gain_ref, router_ref, ids_ref, sems
):
    pairs = (
        (hidden_hbm, hidden_ref),
        (gain_hbm, gain_ref),
        (router_hbm, router_ref),
        (ids_hbm, ids_ref),
    )
    copies = [pltpu.make_async_copy(x, y, sems.at[i]) for i, (x, y) in enumerate(pairs)]
    for c in copies:
        c.start()
    for c in copies:
        c.wait()
    rows, width = hidden_ref.shape
    experts = router_ref.shape[0]
    lanes = packet_ref.shape[1] - width
    values = hidden_ref[...].astype(F32)
    spread = jnp.mean(values * values, axis=-1, keepdims=True)
    normed = (values * lax.rsqrt(spread + 1e-06) * gain_ref[...]).astype(BF16)
    packet_ref[:, :width] = normed
    logits = lax.dot_general(
        router_ref[...], normed, (((1,), (1,)), ((), ())), preferred_element_type=F32
    )
    probs = 1.0 / (1.0 + jnp.exp(-logits))
    live = (iota((1, rows), 1) < live_ref[0]).astype(F32)
    seats = iota((experts, rows), 0)
    named = jnp.zeros((experts, rows), F32)
    for k in range(ids_ref.shape[0]):
        named = named + (ids_ref[k : k + 1, :] == seats).astype(F32)
    picked = named * probs
    weights = (live * picked / jnp.sum(picked, axis=0, keepdims=True)).astype(BF16)
    taken = named * live
    earlier = (iota((rows, rows), 0) < iota((rows, rows), 1)).astype(F32).astype(BF16)
    slot = jnp.dot(taken.astype(BF16), earlier, preferred_element_type=F32)
    code = (taken * (slot + 1.0)).astype(BF16)
    load = jnp.sum(taken, axis=1, keepdims=True).astype(BF16)
    mass = jnp.sum(probs * live, axis=1, keepdims=True)
    meta = jnp.zeros((rows, lanes), F32)
    for at, piece in enumerate([weights, code, load, *split_three(mass)]):
        put = iota((experts, lanes), 1) == iota((experts, lanes), 0) + at * experts
        piece = jnp.broadcast_to(piece.astype(F32), (experts, rows)).astype(BF16)
        meta = meta + lax.dot_general(
            piece,
            put.astype(F32).astype(BF16),
            (((0,), (0,)), ((), ())),
            preferred_element_type=F32,
        )
    packet_ref[:, width:] = meta.astype(BF16)


def columns_of(block_ref, width, at):
    notes = block_ref[:, width:].astype(F32)
    lane = iota(notes.shape, 1)
    return [jnp.sum(jnp.where(lane == a, notes, 0.0), axis=1, keepdims=True) for a in at]


def matches(block_ref, width, experts, capacity):
    me, peer = my_seat()
    rows = block_ref.shape[0]
    mine, theirs = columns_of(block_ref, width, [experts + me, experts + peer])
    slot = iota((rows, 2 * capacity), 1)
    place = jnp.where(slot < capacity, mine, theirs).astype(jnp.int32)
    return (place - 1) == jnp.where(slot < capacity, slot, slot - capacity), slot


def pick_kernel(count, width, experts, capacity, *refs):
    blocks, (mine_ref, peer_ref) = refs[:count], refs[count:]
    sums = []
    for i, block in enumerate(blocks):
        match, _ = matches(block, width, experts, capacity)
        rows = lax.dot_general(
            match.astype(F32).astype(BF16),
            block[:, :width],
            (((0,), (0,)), ((), ())),
            preferred_element_type=F32,
        ).astype(BF16)
        mine_ref[i * capacity : (i + 1) * capacity, :] = rows[:capacity]
        peer_ref[i * capacity : (i + 1) * capacity, :] = rows[capacity:]
        sums.append(block[0:1, width:].astype(F32))
    filler = jnp.zeros((16 - count, sums[0].shape[1]), F32)
    sums = jnp.concatenate(sums + [filler], axis=0).astype(BF16)
    for ref in (mine_ref, peer_ref):
        ref[count * capacity :, : sums.shape[1]] = sums


def silu(value):
    return value / (1.0 + jnp.exp(-value))


def load_kernel(*refs):
    count = (len(refs) - 1) // 2
    sems = refs[-1]
    copies = [pltpu.make_async_copy(refs[i], refs[count + i], sems.at[i]) for i in range(count)]
    for c in copies:
        c.start()
    for c in copies:
        c.wait()


def expert_kernel(mine_ref, peer_ref, up_ref, down_ref, mine_out, peer_out, active):
    half, width = mine_out.shape
    units = down_ref.shape[0]
    rows = jnp.concatenate([mine_ref[:half, :], peer_ref[:half, :]], axis=0)
    for at in range(0, units, 256):
        to = min(at + 256, units)
        gate = jnp.dot(rows, up_ref[:, at:to], preferred_element_type=F32)
        up = jnp.dot(rows, up_ref[:, units + at : units + to], preferred_element_type=F32)
        active[:, at:to] = (silu(gate) * up).astype(BF16)
    for at in range(0, width, 512):
        to = min(at + 512, width)
        result = jnp.dot(active[...], down_ref[:, at:to], preferred_element_type=F32).astype(BF16)
        mine_out[:, at:to] = result[:half]
        peer_out[:, at:to] = result[half:]


def shared_kernel(count, width, *refs):
    blocks, (weights_ref, out_ref) = refs[:count], refs[count:]
    states = jnp.concatenate([b[:, :width] for b in blocks], axis=0)
    across = (((1,), (1,)), ((), ()))
    gate = lax.dot_general(states, weights_ref[0], across, preferred_element_type=F32)
    up = lax.dot_general(states, weights_ref[1], across, preferred_element_type=F32)
    active = (silu(gate) * up).astype(BF16)
    out_ref[...] = jnp.dot(active, weights_ref[2], preferred_element_type=F32)


def mix_kernel(count, width, experts, capacity, *refs):
    blocks, (mine_ref, peer_ref, shared_ref), outs = refs[:count], refs[count : count + 3], refs[count + 3 :]
    me, peer = my_seat()
    rows = blocks[0].shape[0]
    for i, block in enumerate(blocks):
        match, slot = matches(block, width, experts, capacity)
        mine, theirs = columns_of(block, width, [me, peer])
        mixing = jnp.where(match, jnp.where(slot < capacity, mine, theirs), 0.0).astype(BF16)
        at = slice(i * capacity, (i + 1) * capacity)
        results = jnp.concatenate([mine_ref[at, :], peer_ref[at, :]], axis=0)
        total = shared_ref[i * rows : (i + 1) * rows, :] + jnp.dot(
            mixing, results, preferred_element_type=F32
        )
        outs[i][...] = total.astype(outs[i].dtype)


def penalty_kernel(experts, scale, steps, *refs):
    sums, out_ref = refs[:-1], refs[-1]
    own = jnp.concatenate([s[...] for s in sums[0::2]], axis=0)
    peer = jnp.concatenate([s[...] for s in sums[1::2]], axis=0)
    seats = own.shape[0]
    seat = lax.axis_index("expert")
    row = iota((seats, seats), 1)
    step = jnp.zeros_like(row)
    for r, k in enumerate(steps):
        step = jnp.where(row == r, k, step)
    order = (iota((seats, seats), 0) == (step ^ seat)).astype(F32).astype(BF16)
    own = jnp.dot(order, own, preferred_element_type=F32)
    peer = jnp.dot(order, peer, preferred_element_type=F32)

    def part(array, i):
        return array[:, i * experts : (i + 1) * experts]

    load = jnp.sum(part(own, 2) + part(peer, 2), axis=0, keepdims=True)
    mass = (part(own, 3) + part(own, 4) + part(own, 5)) + (part(peer, 3) + part(peer, 4) + part(peer, 5))
    mass = jnp.sum(mass, axis=0, keepdims=True)
    out_ref[...] = jnp.sum(load * mass, axis=1, keepdims=True) * experts / scale


def call(kernel, out_shape, where, flops, nbytes, mib, scratch=()):
    spaces = {"v": pltpu.VMEM, "s": pltpu.SMEM, "h": pltpu.HBM}
    many = isinstance(out_shape, (list, tuple))
    specs = {"v": VMEM, "s": SMEM, "h": pl.BlockSpec(memory_space=pltpu.HBM)}

    def vmem(x):
        return pltpu.VMEM(x.shape, x.dtype)

    run = pl.pallas_call(
        kernel,
        out_shape=[vmem(x) for x in out_shape] if many else vmem(out_shape),
        in_specs=[specs[w] for w in where],
        out_specs=[VMEM] * len(out_shape) if many else VMEM,
        scratch_shapes=list(scratch),
        cost_estimate=pl.CostEstimate(flops=flops, bytes_accessed=nbytes, transcendentals=0),
        compiler_params=pltpu.CompilerParams(vmem_limit_bytes=mib << 20),
    )

    def go(*args):
        args = [
            a if w == "s" else pltpu.with_memory_space_constraint(a, spaces[w])
            for a, w in zip(args, where)
        ]
        return run(*args)

    return go


def chunks_of(steps):
    return [[0], list(range(1, steps - 1)), [steps - 1]]


def sent_as(step):
    return {0: (F32, F32), 1: (BF16, BF16)}.get(step, (F32, BF16))


def on_device(
    hidden_state,
    norm_gain,
    router_weight,
    expert_ids,
    live_counts,
    routed_gate_up,
    routed_down,
    shared_weights,
):
    tok_rows, width = hidden_state.shape
    choose = expert_ids.shape[1]
    hidden_units = routed_down.shape[1]
    expert_count = lax.axis_size("expert")
    sub_count = lax.axis_size("sub")
    devices = expert_count * sub_count
    all_experts = routed_gate_up.shape[0] * devices
    assert routed_gate_up.shape[0] == 1 and sub_count == 2
    all_tokens = tok_rows * devices
    capacity = (tok_rows * choose * 4 + 3 * all_experts - 1) // (3 * all_experts)
    shape = jax.ShapeDtypeStruct

    def cross(block, step):
        return lax.ppermute(block, "expert", [(e, e ^ step) for e in range(expert_count)])

    def swap(block):
        return lax.ppermute(block, "sub", [(0, 1), (1, 0)])

    lanes = -(-6 * all_experts // 128) * 128
    packet = call(
        route_kernel,
        shape((tok_rows, width + lanes), BF16),
        "shhhh",
        2 * tok_rows * width * all_experts,
        4 * tok_rows * width,
        8,
        [
            pltpu.VMEM((tok_rows, width), BF16),
            pltpu.VMEM((1, width), F32),
            pltpu.VMEM((all_experts, width), BF16),
            pltpu.VMEM((choose, tok_rows), jnp.int32),
            pltpu.SemaphoreType.DMA((4,)),
        ],
    )(live_counts, hidden_state, norm_gain.reshape(1, width), router_weight.T, expert_ids.T)

    steps = expert_count // 2
    chunks = chunks_of(steps)
    direct = [packet, cross(packet, 2)]
    for j in range(2, steps):
        direct.append(cross(direct[j - 1], 2) if j % 2 else cross(packet, 2 * j))
    near = [cross(packet, 1)]
    near.append(cross(near[0], 2))
    near += [cross(direct[j], 1) for j in range(2, steps)]

    def load(*arrays):
        return call(
            load_kernel,
            [shape(a.shape, a.dtype) for a in arrays],
            "h" * len(arrays),
            0,
            sum(2 * a.size for a in arrays),
            1,
            [pltpu.SemaphoreType.DMA((len(arrays),))],
        )(*arrays)

    (gate_up,) = load(routed_gate_up[0])
    down, shared_rows = load(routed_down[0], jnp.swapaxes(shared_weights, 1, 2))
    keeps, leaves, sums = [None] * steps, [None] * steps, []
    for chunk in chunks:
        blocks = [b for j in chunk for b in (direct[j], near[j])]
        count = len(blocks)
        picked = shape((count * capacity + 16, width), BF16)
        results = shape((count * capacity, width), BF16)
        mine, theirs = call(
            functools.partial(pick_kernel, count, width, all_experts, capacity),
            (picked, picked),
            "v" * count,
            4 * count * tok_rows * capacity * width,
            8 * count * capacity * width,
            8,
        )(*blocks)
        theirs = swap(theirs)
        shared = call(
            functools.partial(shared_kernel, count, width),
            shape((count * tok_rows, width), F32),
            "v" * (count + 1),
            6 * count * tok_rows * width * shared_rows.shape[1],
            6 * width * shared_rows.shape[1],
            8,
        )(*blocks, shared_rows)
        sums += [x[count * capacity :][:count, :lanes] for x in (mine, theirs)]
        mine, theirs = call(
            expert_kernel,
            (results, results),
            "vvvv",
            12 * count * capacity * width * hidden_units,
            6 * width * hidden_units,
            8,
            [pltpu.VMEM((2 * count * capacity, hidden_units), BF16)],
        )(mine, theirs, gate_up, down)
        theirs = swap(theirs)
        tokens = (tok_rows, width)
        totals = call(
            functools.partial(mix_kernel, count, width, all_experts, capacity),
            [shape(tokens, t) for j in chunk for t in sent_as(j)],
            "v" * (count + 3),
            4 * count * tok_rows * capacity * width,
            8 * count * tok_rows * width,
            8,
        )(*blocks, mine, theirs, shared)
        for i, j in enumerate(chunk):
            keeps[j], leaves[j] = totals[2 * i], totals[2 * i + 1]

    other = leaves[0] + cross(leaves[1], 2).astype(F32)
    mixed = keeps[0] + cross(keeps[1], 2).astype(F32)
    for j in range(2, steps):
        both = keeps[j] + cross(leaves[j], 1).astype(F32)
        mixed = mixed + cross(both.astype(BF16), 2 * j).astype(F32)
    mixed = (mixed + cross(other.astype(BF16), 1).astype(F32)).astype(BF16)

    penalty = call(
        functools.partial(
            penalty_kernel,
            all_experts,
            choose * float(all_tokens) * float(all_tokens),
            [2 * j + b for chunk in chunks for j in chunk for b in range(2)],
        ),
        shape((1, 1), F32),
        "v" * len(sums),
        0,
        0,
        4,
    )(*sums)
    return (mixed, penalty.reshape(1))


def solution(mesh):
    placed = (
        P(("groups", "expert", "sub"), None),
        P(),
        P(),
        P(("groups", "expert", "sub"), None),
        P(("groups", "expert", "sub")),
        P(("expert", "sub"), None, None),
        P(("expert", "sub"), None, None),
        P(None, None, "expert"),
    )

    return jax.shard_map(
        on_device,
        mesh=mesh,
        in_specs=placed,
        out_specs=(P(("groups", "expert", "sub"), None), P("groups")),
        check_vma=False,
    )
```

```python
import functools

import jax
import jax.numpy as jnp
from jax import lax
from jax.experimental import pallas as pl
from jax.experimental.pallas import tpu as pltpu
from jax.sharding import PartitionSpec as P


F32 = jnp.float32
BF16 = jnp.bfloat16
VMEM = pl.BlockSpec(memory_space=pltpu.VMEM)
SMEM = pl.BlockSpec(memory_space=pltpu.SMEM)
ANY = pl.BlockSpec(memory_space=pl.ANY)


def split_three(values):
    high = values.astype(BF16)
    rest = values - high.astype(F32)
    middle = rest.astype(BF16)
    low = (rest - middle.astype(F32)).astype(BF16)
    return high, middle, low


def iota(shape, axis):
    return lax.broadcasted_iota(jnp.int32, shape, axis)


def my_seat():
    me = lax.axis_index("expert") * 2 + lax.axis_index("sub")
    return me, me ^ 1


def route_kernel(
    live_ref, hidden_hbm, gain_hbm, router_hbm, ids_hbm, packet_ref, hidden_ref, gain_ref, router_ref, ids_ref, sems
):
    pairs = (
        (hidden_hbm, hidden_ref),
        (gain_hbm, gain_ref),
        (router_hbm, router_ref),
        (ids_hbm, ids_ref),
    )
    copies = [pltpu.make_async_copy(x, y, sems.at[i]) for i, (x, y) in enumerate(pairs)]
    for c in copies:
        c.start()
    for c in copies:
        c.wait()
    rows, width = hidden_ref.shape
    experts = router_ref.shape[0]
    lanes = packet_ref.shape[1] - width
    values = hidden_ref[...].astype(F32)
    spread = jnp.mean(values * values, axis=-1, keepdims=True)
    normed = (values * lax.rsqrt(spread + 1e-06) * gain_ref[...]).astype(BF16)
    packet_ref[:, :width] = normed
    logits = lax.dot_general(
        router_ref[...], normed, (((1,), (1,)), ((), ())), preferred_element_type=F32
    )
    probs = 1.0 / (1.0 + jnp.exp(-logits))
    live = (iota((1, rows), 1) < live_ref[0]).astype(F32)
    seats = iota((experts, rows), 0)
    named = jnp.zeros((experts, rows), F32)
    for k in range(ids_ref.shape[0]):
        named = named + (ids_ref[k : k + 1, :] == seats).astype(F32)
    picked = named * probs
    weights = (live * picked / jnp.sum(picked, axis=0, keepdims=True)).astype(BF16)
    taken = named * live
    earlier = (iota((rows, rows), 0) < iota((rows, rows), 1)).astype(F32).astype(BF16)
    slot = jnp.dot(taken.astype(BF16), earlier, preferred_element_type=F32)
    code = (taken * (slot + 1.0)).astype(BF16)
    load = jnp.sum(taken, axis=1, keepdims=True).astype(BF16)
    mass = jnp.sum(probs * live, axis=1, keepdims=True)
    meta = jnp.zeros((rows, lanes), F32)
    for at, piece in enumerate([weights, code, load, *split_three(mass)]):
        put = iota((experts, lanes), 1) == iota((experts, lanes), 0) + at * experts
        piece = jnp.broadcast_to(piece.astype(F32), (experts, rows)).astype(BF16)
        meta = meta + lax.dot_general(
            piece,
            put.astype(F32).astype(BF16),
            (((0,), (0,)), ((), ())),
            preferred_element_type=F32,
        )
    packet_ref[:, width:] = meta.astype(BF16)


def columns_of(block_ref, width, at):
    notes = block_ref[:, width:].astype(F32)
    lane = iota(notes.shape, 1)
    return [jnp.sum(jnp.where(lane == a, notes, 0.0), axis=1, keepdims=True) for a in at]


def matches(block_ref, width, experts, capacity):
    me, peer = my_seat()
    rows = block_ref.shape[0]
    mine, theirs = columns_of(block_ref, width, [experts + me, experts + peer])
    slot = iota((rows, 2 * capacity), 1)
    place = jnp.where(slot < capacity, mine, theirs).astype(jnp.int32)
    return (place - 1) == jnp.where(slot < capacity, slot, slot - capacity), slot


def pick_kernel(count, width, experts, capacity, *refs):
    blocks, (mine_ref, peer_ref) = refs[:count], refs[count:]
    sums = []
    for i, block in enumerate(blocks):
        match, _ = matches(block, width, experts, capacity)
        rows = lax.dot_general(
            match.astype(F32).astype(BF16),
            block[:, :width],
            (((0,), (0,)), ((), ())),
            preferred_element_type=F32,
        ).astype(BF16)
        mine_ref[i * capacity : (i + 1) * capacity, :] = rows[:capacity]
        peer_ref[i * capacity : (i + 1) * capacity, :] = rows[capacity:]
        sums.append(block[0:1, width:].astype(F32))
    filler = jnp.zeros((16 - count, sums[0].shape[1]), F32)
    sums = jnp.concatenate(sums + [filler], axis=0).astype(BF16)
    for ref in (mine_ref, peer_ref):
        ref[count * capacity :, : sums.shape[1]] = sums


def silu(value):
    return value / (1.0 + jnp.exp(-value))


def load_kernel(*refs):
    count = (len(refs) - 1) // 2
    sems = refs[-1]
    copies = [pltpu.make_async_copy(refs[i], refs[count + i], sems.at[i]) for i in range(count)]
    for c in copies:
        c.start()
    for c in copies:
        c.wait()


def expert_kernel(mine_ref, peer_ref, up_ref, down_ref, mine_out, peer_out, active):
    half, width = mine_out.shape
    units = down_ref.shape[0]
    rows = jnp.concatenate([mine_ref[:half, :], peer_ref[:half, :]], axis=0)
    for at in range(0, units, 256):
        to = min(at + 256, units)
        gate = jnp.dot(rows, up_ref[:, at:to], preferred_element_type=F32)
        up = jnp.dot(rows, up_ref[:, units + at : units + to], preferred_element_type=F32)
        active[:, at:to] = (silu(gate) * up).astype(BF16)
    for at in range(0, width, 512):
        to = min(at + 512, width)
        result = jnp.dot(active[...], down_ref[:, at:to], preferred_element_type=F32).astype(BF16)
        mine_out[:, at:to] = result[:half]
        peer_out[:, at:to] = result[half:]


def shared_kernel(count, width, *refs):
    blocks, weights_ref, outs = refs[:count], refs[count], refs[count + 1 :]
    states = jnp.concatenate([b[:, :width] for b in blocks], axis=0)
    across = (((1,), (1,)), ((), ()))
    gate = lax.dot_general(states, weights_ref[0], across, preferred_element_type=F32)
    up = lax.dot_general(states, weights_ref[1], across, preferred_element_type=F32)
    active = (silu(gate) * up).astype(BF16)
    at = 0
    for out in outs:
        rows = active[at : at + out.shape[0]]
        out[...] = jnp.dot(rows, weights_ref[2], preferred_element_type=F32)
        at += out.shape[0]


def mix_kernel(count, width, experts, capacity, cuts, *refs):
    blocks, (mine_ref, peer_ref, shared_ref) = refs[:count], refs[count : count + 3]
    outs, at = [], count + 3
    for pieces in cuts:
        outs.append(refs[at : at + pieces])
        at += pieces
    me, peer = my_seat()
    rows = blocks[0].shape[0]
    for i, block in enumerate(blocks):
        match, slot = matches(block, width, experts, capacity)
        mine, theirs = columns_of(block, width, [me, peer])
        mixing = jnp.where(match, jnp.where(slot < capacity, mine, theirs), 0.0).astype(BF16)
        at = slice(i * capacity, (i + 1) * capacity)
        results = jnp.concatenate([mine_ref[at, :], peer_ref[at, :]], axis=0)
        total = shared_ref[i * rows : (i + 1) * rows, :] + jnp.dot(
            mixing, results, preferred_element_type=F32
        )
        at = 0
        for out in outs[i]:
            out[...] = total[:, at : at + out.shape[1]].astype(out.dtype)
            at += out.shape[1]


def add_kernel(keep_ref, more_ref, out_ref):
    out_ref[...] = (keep_ref[...] + more_ref[...].astype(F32)).astype(out_ref.dtype)


def sum_kernel(*refs):
    pieces, out_ref = refs[:-1], refs[-1]
    total, at, width = None, 0, out_ref.shape[1]
    sums = []
    for piece in pieces:
        sums.append((at, piece[...].astype(F32)))
        at = (at + piece.shape[1]) % width
    whole = [x for _, x in sums if x.shape[1] == width]
    total = functools.reduce(lambda x, y: x + y, whole)
    for at, x in sums:
        if x.shape[1] < width:
            to = at + x.shape[1]
            out_ref[:, at:to] = (total[:, at:to] + x).astype(out_ref.dtype)


def penalty_kernel(experts, scale, steps, *refs):
    sums, out_ref = refs[:-1], refs[-1]
    own = jnp.concatenate([s[...] for s in sums[0::2]], axis=0)
    peer = jnp.concatenate([s[...] for s in sums[1::2]], axis=0)
    seats = own.shape[0]
    seat = lax.axis_index("expert")
    row = iota((seats, seats), 1)
    step = jnp.zeros_like(row)
    for r, k in enumerate(steps):
        step = jnp.where(row == r, k, step)
    order = (iota((seats, seats), 0) == (step ^ seat)).astype(F32).astype(BF16)
    own = jnp.dot(order, own, preferred_element_type=F32)
    peer = jnp.dot(order, peer, preferred_element_type=F32)

    def part(array, i):
        return array[:, i * experts : (i + 1) * experts]

    load = jnp.sum(part(own, 2) + part(peer, 2), axis=0, keepdims=True)
    mass = (part(own, 3) + part(own, 4) + part(own, 5)) + (part(peer, 3) + part(peer, 4) + part(peer, 5))
    mass = jnp.sum(mass, axis=0, keepdims=True)
    out_ref[...] = jnp.sum(load * mass, axis=1, keepdims=True) * experts / scale


def call(kernel, out_shape, where, flops, nbytes, mib, scratch=(), out="v"):
    spaces = {"v": pltpu.VMEM, "s": pltpu.SMEM, "h": pltpu.HBM}
    many = isinstance(out_shape, (list, tuple))
    specs = {"v": VMEM, "s": SMEM, "h": pl.BlockSpec(memory_space=pltpu.HBM)}

    def vmem(x):
        return pltpu.VMEM(x.shape, x.dtype) if out == "v" else x

    run = pl.pallas_call(
        kernel,
        out_shape=[vmem(x) for x in out_shape] if many else vmem(out_shape),
        in_specs=[specs[w] for w in where],
        out_specs=[VMEM] * len(out_shape) if many else VMEM,
        scratch_shapes=list(scratch),
        cost_estimate=pl.CostEstimate(flops=flops, bytes_accessed=nbytes, transcendentals=0),
        compiler_params=pltpu.CompilerParams(vmem_limit_bytes=mib << 20),
    )

    def go(*args):
        args = [
            a if w == "s" else pltpu.with_memory_space_constraint(a, spaces[w])
            for a, w in zip(args, where)
        ]
        return run(*args)

    return go


def chunks_of(steps):
    return [[0], list(range(2, steps, 2)), list(range(1, steps, 2))]


def sent_as(step):
    return {0: (F32, F32), 1: (BF16, BF16)}.get(step, (F32, BF16))


def pieces_of(step, steps):
    return 2 if step == steps - 1 else 1


def on_device(
    hidden_state,
    norm_gain,
    router_weight,
    expert_ids,
    live_counts,
    routed_gate_up,
    routed_down,
    shared_weights,
):
    tok_rows, width = hidden_state.shape
    choose = expert_ids.shape[1]
    hidden_units = routed_down.shape[1]
    expert_count = lax.axis_size("expert")
    sub_count = lax.axis_size("sub")
    devices = expert_count * sub_count
    all_experts = routed_gate_up.shape[0] * devices
    assert routed_gate_up.shape[0] == 1 and sub_count == 2
    all_tokens = tok_rows * devices
    capacity = (tok_rows * choose * 4 + 3 * all_experts - 1) // (3 * all_experts)
    shape = jax.ShapeDtypeStruct

    def cross(block, step):
        return lax.ppermute(block, "expert", [(e, e ^ step) for e in range(expert_count)])

    def swap(block):
        return lax.ppermute(block, "sub", [(0, 1), (1, 0)])

    lanes = -(-6 * all_experts // 128) * 128
    packet = call(
        route_kernel,
        shape((tok_rows, width + lanes), BF16),
        "shhhh",
        2 * tok_rows * width * all_experts,
        4 * tok_rows * width,
        8,
        [
            pltpu.VMEM((tok_rows, width), BF16),
            pltpu.VMEM((1, width), F32),
            pltpu.VMEM((all_experts, width), BF16),
            pltpu.VMEM((choose, tok_rows), jnp.int32),
            pltpu.SemaphoreType.DMA((4,)),
        ],
    )(live_counts, hidden_state, norm_gain.reshape(1, width), router_weight.T, expert_ids.T)

    steps = expert_count // 2
    chunks = chunks_of(steps)
    direct = [packet, cross(packet, 2)]
    for j in range(2, steps):
        direct.append(cross(direct[j - 1], 2) if j % 2 else cross(packet, 2 * j))
    near = [cross(packet, 1)]
    near.append(cross(near[0], 2))
    near += [cross(direct[j], 1) for j in range(2, steps)]

    def load(*arrays):
        return call(
            load_kernel,
            [shape(a.shape, a.dtype) for a in arrays],
            "h" * len(arrays),
            0,
            sum(2 * a.size for a in arrays),
            1,
            [pltpu.SemaphoreType.DMA((len(arrays),))],
        )(*arrays)

    (gate_up,) = load(routed_gate_up[0])
    down, shared_rows = load(routed_down[0], jnp.swapaxes(shared_weights, 1, 2))
    arrived = [(direct[j], near[j]) for j in range(steps)]

    def shared_sums(chunks):
        blocks = [b for chunk in chunks for j in chunk for b in arrived[j]]
        return call(
            functools.partial(shared_kernel, len(blocks), width),
            [shape((2 * len(chunk) * tok_rows, width), F32) for chunk in chunks],
            "v" * (len(blocks) + 1),
            6 * len(blocks) * tok_rows * width * shared_rows.shape[1],
            6 * width * shared_rows.shape[1],
            8,
        )(*blocks, shared_rows)

    shared = shared_sums(chunks[:2]) + shared_sums(chunks[2:])
    keeps, leaves, sums = [None] * steps, [None] * steps, []
    for c, chunk in enumerate(chunks):
        blocks = [b for j in chunk for b in arrived[j]]
        count = len(blocks)
        picked = shape((count * capacity + 16, width), BF16)
        results = shape((count * capacity, width), BF16)
        mine, theirs = call(
            functools.partial(pick_kernel, count, width, all_experts, capacity),
            (picked, picked),
            "v" * count,
            4 * count * tok_rows * capacity * width,
            8 * count * capacity * width,
            8,
        )(*blocks)
        theirs = swap(theirs)
        sums += [x[count * capacity :][:count, :lanes] for x in (mine, theirs)]
        mine, theirs = call(
            expert_kernel,
            (results, results),
            "vvvv",
            12 * count * capacity * width * hidden_units,
            6 * width * hidden_units,
            8,
            [pltpu.VMEM((2 * count * capacity, hidden_units), BF16)],
        )(mine, theirs, gate_up, down)
        theirs = swap(theirs)
        cuts = [pieces_of(j, steps) for j in chunk for _ in range(2)]
        kinds = [t for j in chunk for t in sent_as(j)]
        totals = call(
            functools.partial(mix_kernel, count, width, all_experts, capacity, cuts),
            [shape((tok_rows, width // n), t) for n, t in zip(cuts, kinds) for _ in range(n)],
            "v" * (count + 3),
            4 * count * tok_rows * capacity * width,
            8 * count * tok_rows * width,
            8,
        )(*blocks, mine, theirs, shared[c])
        for j in chunk:
            pieces = pieces_of(j, steps)
            keeps[j], leaves[j], totals = totals[:pieces], totals[pieces : 2 * pieces], totals[2 * pieces :]

    def add(keep, more):
        return call(add_kernel, shape(keep.shape, BF16), "vv", 0, 0, 4)(keep, more)

    other = add(leaves[0][0], cross(leaves[1][0], 2))
    terms = [keeps[0][0], cross(keeps[1][0], 2)]
    for j in range(2, steps):
        for keep, leave in zip(keeps[j], leaves[j]):
            both = add(keep, cross(leave, 1))
            terms.append(cross(both, 2 * j))
    terms.append(cross(other, 1))
    mixed = call(sum_kernel, shape((tok_rows, width), BF16), "v" * len(terms), 0, 0, 8, out="h")(*terms)

    penalty = call(
        functools.partial(
            penalty_kernel,
            all_experts,
            choose * float(all_tokens) * float(all_tokens),
            [2 * j + b for chunk in chunks for j in chunk for b in range(2)],
        ),
        shape((1, 1), F32),
        "v" * len(sums),
        0,
        0,
        4,
    )(*sums)
    return (mixed, penalty.reshape(1))


def solution(mesh):
    placed = (
        P(("groups", "expert", "sub"), None),
        P(),
        P(),
        P(("groups", "expert", "sub"), None),
        P(("groups", "expert", "sub")),
        P(("expert", "sub"), None, None),
        P(("expert", "sub"), None, None),
        P(None, None, "expert"),
    )

    return jax.shard_map(
        on_device,
        mesh=mesh,
        in_specs=placed,
        out_specs=(P(("groups", "expert", "sub"), None), P("groups")),
        check_vma=False,
    )
```

```python
import functools

import jax
import jax.numpy as jnp
from jax import lax
from jax.experimental import pallas as pl
from jax.experimental.pallas import tpu as pltpu
from jax.sharding import PartitionSpec as P


F32 = jnp.float32
BF16 = jnp.bfloat16
HALVES = 2
VMEM = pl.BlockSpec(memory_space=pltpu.VMEM)
SMEM = pl.BlockSpec(memory_space=pltpu.SMEM)
ANY = pl.BlockSpec(memory_space=pl.ANY)


def split_three(values):
    high = values.astype(BF16)
    rest = values - high.astype(F32)
    middle = rest.astype(BF16)
    low = (rest - middle.astype(F32)).astype(BF16)
    return high, middle, low


def iota(shape, axis):
    return lax.broadcasted_iota(jnp.int32, shape, axis)


def my_seat():
    me = lax.axis_index("expert") * 2 + lax.axis_index("sub")
    return me, me ^ 1


def route_kernel(live_ref, hidden_hbm, gain_hbm, router_hbm, ids_hbm, packet_ref, *more):
    *piece_refs, hidden_ref, gain_ref, router_ref, ids_ref, sems = more
    pairs = (
        (hidden_hbm, hidden_ref),
        (gain_hbm, gain_ref),
        (router_hbm, router_ref),
        (ids_hbm, ids_ref),
    )
    copies = [pltpu.make_async_copy(x, y, sems.at[i]) for i, (x, y) in enumerate(pairs)]
    for c in copies:
        c.start()
    for c in copies:
        c.wait()
    rows, width = hidden_ref.shape
    experts = router_ref.shape[0]
    lanes = packet_ref.shape[1] - width
    values = hidden_ref[...].astype(F32)
    spread = jnp.mean(values * values, axis=-1, keepdims=True)
    normed = (values * lax.rsqrt(spread + 1e-06) * gain_ref[...]).astype(BF16)
    packet_ref[:, :width] = normed
    logits = lax.dot_general(
        router_ref[...], normed, (((1,), (1,)), ((), ())), preferred_element_type=F32
    )
    probs = 1.0 / (1.0 + jnp.exp(-logits))
    live = (iota((1, rows), 1) < live_ref[0]).astype(F32)
    seats = iota((experts, rows), 0)
    named = jnp.zeros((experts, rows), F32)
    for k in range(ids_ref.shape[0]):
        named = named + (ids_ref[k : k + 1, :] == seats).astype(F32)
    picked = named * probs
    weights = (live * picked / jnp.sum(picked, axis=0, keepdims=True)).astype(BF16)
    taken = named * live
    earlier = (iota((rows, rows), 0) < iota((rows, rows), 1)).astype(F32).astype(BF16)
    slot = jnp.dot(taken.astype(BF16), earlier, preferred_element_type=F32)
    code = (taken * (slot + 1.0)).astype(BF16)
    load = jnp.sum(taken, axis=1, keepdims=True).astype(BF16)
    mass = jnp.sum(probs * live, axis=1, keepdims=True)
    meta = jnp.zeros((rows, lanes), F32)
    for at, piece in enumerate([weights, code, load, *split_three(mass)]):
        put = iota((experts, lanes), 1) == iota((experts, lanes), 0) + at * experts
        piece = jnp.broadcast_to(piece.astype(F32), (experts, rows)).astype(BF16)
        meta = meta + lax.dot_general(
            piece,
            put.astype(F32).astype(BF16),
            (((0,), (0,)), ((), ())),
            preferred_element_type=F32,
        )
    packet_ref[:, width:] = meta.astype(BF16)
    at = 0
    for piece in piece_refs:
        to = at + piece.shape[0]
        piece[:, :width] = normed[at:to]
        piece[:, width:] = meta[at:to].astype(BF16)
        at = to


def packets_of(refs, pieces):
    packets, at = [], 0
    for count in pieces:
        parts = [ref[...] for ref in refs[at : at + count]]
        packets.append(parts[0] if count == 1 else jnp.concatenate(parts, axis=0))
        at += count
    return packets, refs[at:]


def columns_of(block, width, at):
    notes = block[:, width:].astype(F32)
    lane = iota(notes.shape, 1)
    return [jnp.sum(jnp.where(lane == a, notes, 0.0), axis=1, keepdims=True) for a in at]


def matches(block, width, experts, capacity):
    me, peer = my_seat()
    rows = block.shape[0]
    mine, theirs = columns_of(block, width, [experts + me, experts + peer])
    slot = iota((rows, 2 * capacity), 1)
    place = jnp.where(slot < capacity, mine, theirs).astype(jnp.int32)
    return (place - 1) == jnp.where(slot < capacity, slot, slot - capacity), slot


def pick_kernel(pieces, width, experts, capacity, *refs):
    blocks, (mine_ref, peer_ref) = packets_of(refs, pieces)
    count = len(blocks)
    sums = []
    for i, block in enumerate(blocks):
        match, _ = matches(block, width, experts, capacity)
        rows = lax.dot_general(
            match.astype(F32).astype(BF16),
            block[:, :width],
            (((0,), (0,)), ((), ())),
            preferred_element_type=F32,
        ).astype(BF16)
        mine_ref[i * capacity : (i + 1) * capacity, :] = rows[:capacity]
        peer_ref[i * capacity : (i + 1) * capacity, :] = rows[capacity:]
        sums.append(block[0:1, width:].astype(F32))
    filler = jnp.zeros((16 - count, sums[0].shape[1]), F32)
    sums = jnp.concatenate(sums + [filler], axis=0).astype(BF16)
    for ref in (mine_ref, peer_ref):
        ref[count * capacity :, : sums.shape[1]] = sums


def silu(value):
    return value / (1.0 + jnp.exp(-value))


def load_kernel(*refs):
    count = (len(refs) - 1) // 2
    sems = refs[-1]
    copies = [pltpu.make_async_copy(refs[i], refs[count + i], sems.at[i]) for i in range(count)]
    for c in copies:
        c.start()
    for c in copies:
        c.wait()


def expert_kernel(start, mine_ref, peer_ref, up_ref, down_ref, mine_out, peer_out, active):
    half, width = mine_out.shape
    units = down_ref.shape[0]
    end = start + half
    rows = jnp.concatenate([mine_ref[start:end, :], peer_ref[start:end, :]], axis=0)
    for at in range(0, units, 256):
        to = min(at + 256, units)
        gate = jnp.dot(rows, up_ref[:, at:to], preferred_element_type=F32)
        up = jnp.dot(rows, up_ref[:, units + at : units + to], preferred_element_type=F32)
        active[:, at:to] = (silu(gate) * up).astype(BF16)
    for at in range(0, width, 512):
        to = min(at + 512, width)
        result = jnp.dot(active[...], down_ref[:, at:to], preferred_element_type=F32).astype(BF16)
        mine_out[:, at:to] = result[:half]
        peer_out[:, at:to] = result[half:]


def shared_kernel(pieces, width, *refs):
    blocks, (weights_ref, *outs) = packets_of(refs, pieces)
    states = jnp.concatenate([b[:, :width] for b in blocks], axis=0)
    across = (((1,), (1,)), ((), ()))
    gate = lax.dot_general(states, weights_ref[0], across, preferred_element_type=F32)
    up = lax.dot_general(states, weights_ref[1], across, preferred_element_type=F32)
    active = (silu(gate) * up).astype(BF16)
    at = 0
    for out in outs:
        rows = active[at : at + out.shape[0]]
        out[...] = jnp.dot(rows, weights_ref[2], preferred_element_type=F32)
        at += out.shape[0]


def mix_kernel(pieces, width, experts, capacity, cuts, *refs):
    blocks, (mine_ref, peer_ref, shared_ref, *out_refs) = packets_of(refs, pieces)
    outs, at = [], 0
    for n in cuts:
        outs.append(out_refs[at : at + n])
        at += n
    me, peer = my_seat()
    rows = blocks[0].shape[0]
    for i, block in enumerate(blocks):
        match, slot = matches(block, width, experts, capacity)
        mine, theirs = columns_of(block, width, [me, peer])
        mixing = jnp.where(match, jnp.where(slot < capacity, mine, theirs), 0.0).astype(BF16)
        at = slice(i * capacity, (i + 1) * capacity)
        results = jnp.concatenate([mine_ref[at, :], peer_ref[at, :]], axis=0)
        total = shared_ref[i * rows : (i + 1) * rows, :] + jnp.dot(
            mixing, results, preferred_element_type=F32
        )
        at = 0
        for out in outs[i]:
            out[...] = total[:, at : at + out.shape[1]].astype(out.dtype)
            at += out.shape[1]


def add_kernel(keep_ref, more_ref, out_ref):
    out_ref[...] = (keep_ref[...] + more_ref[...].astype(F32)).astype(out_ref.dtype)


def sum_kernel(*refs):
    terms, out_ref = refs[:-1], refs[-1]
    width = out_ref.shape[1]
    narrow = min(term.shape[1] for term in terms)
    starts, at = [], 0
    for term in terms:
        starts.append(at)
        at = (at + term.shape[1]) % width
    for left in range(0, width, narrow):
        total = None
        for start, term in zip(starts, terms):
            if start <= left < start + term.shape[1]:
                piece = term[:, left - start : left - start + narrow].astype(F32)
                total = piece if total is None else total + piece
        out_ref[:, left : left + narrow] = total.astype(out_ref.dtype)


def penalty_kernel(experts, scale, steps, *refs):
    sums, out_ref = refs[:-1], refs[-1]
    own = jnp.concatenate([s[...] for s in sums[0::2]], axis=0)
    peer = jnp.concatenate([s[...] for s in sums[1::2]], axis=0)
    seats = own.shape[0]
    seat = lax.axis_index("expert")
    row = iota((seats, seats), 1)
    step = jnp.zeros_like(row)
    for r, k in enumerate(steps):
        step = jnp.where(row == r, k, step)
    order = (iota((seats, seats), 0) == (step ^ seat)).astype(F32).astype(BF16)
    own = jnp.dot(order, own, preferred_element_type=F32)
    peer = jnp.dot(order, peer, preferred_element_type=F32)

    def part(array, i):
        return array[:, i * experts : (i + 1) * experts]

    load = jnp.sum(part(own, 2) + part(peer, 2), axis=0, keepdims=True)
    mass = (part(own, 3) + part(own, 4) + part(own, 5)) + (part(peer, 3) + part(peer, 4) + part(peer, 5))
    mass = jnp.sum(mass, axis=0, keepdims=True)
    out_ref[...] = jnp.sum(load * mass, axis=1, keepdims=True) * experts / scale


def call(kernel, out_shape, where, flops, nbytes, mib, scratch=(), out="v"):
    spaces = {"v": pltpu.VMEM, "s": pltpu.SMEM, "h": pltpu.HBM}
    many = isinstance(out_shape, (list, tuple))
    specs = {"v": VMEM, "s": SMEM, "h": pl.BlockSpec(memory_space=pltpu.HBM)}

    def vmem(x):
        return pltpu.VMEM(x.shape, x.dtype) if out == "v" else x

    run = pl.pallas_call(
        kernel,
        out_shape=[vmem(x) for x in out_shape] if many else vmem(out_shape),
        in_specs=[specs[w] for w in where],
        out_specs=[VMEM] * len(out_shape) if many else VMEM,
        scratch_shapes=list(scratch),
        cost_estimate=pl.CostEstimate(flops=flops, bytes_accessed=nbytes, transcendentals=0),
        compiler_params=pltpu.CompilerParams(vmem_limit_bytes=mib << 20),
    )

    def go(*args):
        args = [
            a if w == "s" else pltpu.with_memory_space_constraint(a, spaces[w])
            for a, w in zip(args, where)
        ]
        return run(*args)

    return go


def chunks_of(steps):
    return [[0], list(range(2, steps, 2)), list(range(3, steps, 2)) + [1]]


def parts_of(chunk):
    return [chunk[:-1], chunk[-1:]] if len(chunk) > 1 and chunk[-1] == 1 else [chunk]


def pieces_of(step, steps):
    return 2 if step == steps - 1 else 1


def on_device(
    hidden_state,
    norm_gain,
    router_weight,
    expert_ids,
    live_counts,
    routed_gate_up,
    routed_down,
    shared_weights,
):
    tok_rows, width = hidden_state.shape
    choose = expert_ids.shape[1]
    hidden_units = routed_down.shape[1]
    expert_count = lax.axis_size("expert")
    sub_count = lax.axis_size("sub")
    devices = expert_count * sub_count
    all_experts = routed_gate_up.shape[0] * devices
    assert routed_gate_up.shape[0] == 1 and sub_count == 2
    all_tokens = tok_rows * devices
    capacity = (tok_rows * choose * 4 + 3 * all_experts - 1) // (3 * all_experts)
    shape = jax.ShapeDtypeStruct

    def cross(block, step):
        return lax.ppermute(block, "expert", [(e, e ^ step) for e in range(expert_count)])

    def swap(block):
        return lax.ppermute(block, "sub", [(0, 1), (1, 0)])

    lanes = -(-6 * all_experts // 128) * 128
    packet, *halves = call(
        route_kernel,
        [shape((tok_rows // n, width + lanes), BF16) for n in (1, HALVES) for _ in range(n)],
        "shhhh",
        2 * tok_rows * width * all_experts,
        4 * tok_rows * width,
        8,
        [
            pltpu.VMEM((tok_rows, width), BF16),
            pltpu.VMEM((1, width), F32),
            pltpu.VMEM((all_experts, width), BF16),
            pltpu.VMEM((choose, tok_rows), jnp.int32),
            pltpu.SemaphoreType.DMA((4,)),
        ],
    )(live_counts, hidden_state, norm_gain.reshape(1, width), router_weight.T, expert_ids.T)

    steps = expert_count // 2
    chunks = chunks_of(steps)

    def cross_all(blocks, step):
        return [cross(b, step) for b in blocks]

    direct, near = [], []
    for j in range(steps):
        if j < 2:
            direct.append([packet] if j == 0 else cross_all([packet], 2))
            near.append(cross_all(direct[j], 1))
        elif j % 2 == 0:
            direct.append(cross_all(halves, 2 * j))
            near.append(cross_all(direct[j], 1))
        else:
            direct.append(cross_all(direct[j - 1], 2))
            near.append(cross_all(near[j - 1], 2))

    def load(*arrays):
        return call(
            load_kernel,
            [shape(a.shape, a.dtype) for a in arrays],
            "h" * len(arrays),
            0,
            sum(2 * a.size for a in arrays),
            1,
            [pltpu.SemaphoreType.DMA((len(arrays),))],
        )(*arrays)

    (gate_up,) = load(routed_gate_up[0])
    (down,) = load(routed_down[0])
    (shared_rows,) = load(jnp.swapaxes(shared_weights, 1, 2))
    arrived = [(direct[j], near[j]) for j in range(steps)]

    keeps, leaves, sums = [None] * steps, [None] * steps, []
    for chunk in chunks:
        blocks = [b for j in chunk for b in arrived[j]]
        pieces = [len(b) for b in blocks]
        flat = [p for b in blocks for p in b]
        count = len(blocks)
        picked = shape((count * capacity + 16, width), BF16)
        mine, theirs = call(
            functools.partial(pick_kernel, pieces, width, all_experts, capacity),
            (picked, picked),
            "v" * len(flat),
            4 * count * tok_rows * capacity * width,
            8 * count * capacity * width,
            8,
        )(*flat)
        theirs = swap(theirs)
        sums += [x[count * capacity :][:count, :lanes] for x in (mine, theirs)]
        parts = parts_of(chunk)
        shared = call(
            functools.partial(shared_kernel, pieces, width),
            [shape((2 * len(steps_in) * tok_rows, width), F32) for steps_in in parts],
            "v" * (len(flat) + 1),
            6 * count * tok_rows * width * shared_rows.shape[1],
            6 * width * shared_rows.shape[1],
            8,
        )(*flat, shared_rows)
        at = 0
        for steps_in, extra in zip(parts, shared):
            count = 2 * len(steps_in)
            results = shape((count * capacity, width), BF16)
            here, away = call(
                functools.partial(expert_kernel, at * capacity),
                (results, results),
                "vvvv",
                12 * count * capacity * width * hidden_units,
                6 * width * hidden_units,
                8,
                [pltpu.VMEM((2 * count * capacity, hidden_units), BF16)],
            )(mine, theirs, gate_up, down)
            away = swap(away)
            cuts = [pieces_of(j, steps) for j in steps_in for _ in range(2)]
            kinds = [F32, BF16] * len(steps_in)
            used = [p for b in blocks[at : at + count] for p in b]
            totals = call(
                functools.partial(mix_kernel, pieces[at : at + count], width, all_experts, capacity, cuts),
                [shape((tok_rows, width // n), t) for n, t in zip(cuts, kinds) for _ in range(n)],
                "v" * (len(used) + 3),
                4 * count * tok_rows * capacity * width,
                8 * count * tok_rows * width,
                8,
            )(*used, here, away, extra)
            for j in steps_in:
                n = pieces_of(j, steps)
                keeps[j], leaves[j], totals = totals[:n], totals[n : 2 * n], totals[2 * n :]
            at = at + count

    terms = [keeps[0][0], cross(leaves[0][0], 1)]
    for j in range(1, steps):
        for keep, leave in zip(keeps[j], leaves[j]):
            more = cross(leave, 1)
            both = call(add_kernel, shape(keep.shape, BF16), "vv", 0, 0, 4)(keep, more)
            terms.append(cross(both, 2 * j))
    mixed = call(sum_kernel, shape((tok_rows, width), BF16), "v" * len(terms), 0, 0, 8, out="h")(*terms)

    penalty = call(
        functools.partial(
            penalty_kernel,
            all_experts,
            choose * float(all_tokens) * float(all_tokens),
            [2 * j + b for chunk in chunks for j in chunk for b in range(2)],
        ),
        shape((1, 1), F32),
        "v" * len(sums),
        0,
        0,
        4,
    )(*sums)
    return (mixed, penalty.reshape(1))


def solution(mesh):
    placed = (
        P(("groups", "expert", "sub"), None),
        P(),
        P(),
        P(("groups", "expert", "sub"), None),
        P(("groups", "expert", "sub")),
        P(("expert", "sub"), None, None),
        P(("expert", "sub"), None, None),
        P(None, None, "expert"),
    )

    return jax.shard_map(
        on_device,
        mesh=mesh,
        in_specs=placed,
        out_specs=(P(("groups", "expert", "sub"), None), P("groups")),
        check_vma=False,
    )
```

```python
import functools

import jax
import jax.numpy as jnp
from jax import lax
from jax.experimental import pallas as pl
from jax.experimental.pallas import tpu as pltpu
from jax.sharding import PartitionSpec as P


F32 = jnp.float32
BF16 = jnp.bfloat16
VMEM = pl.BlockSpec(memory_space=pltpu.VMEM)
SMEM = pl.BlockSpec(memory_space=pltpu.SMEM)
ANY = pl.BlockSpec(memory_space=pl.ANY)


def split_three(values):
    high = values.astype(BF16)
    rest = values - high.astype(F32)
    middle = rest.astype(BF16)
    low = (rest - middle.astype(F32)).astype(BF16)
    return high, middle, low


def iota(shape, axis):
    return lax.broadcasted_iota(jnp.int32, shape, axis)


def my_seat():
    me = lax.axis_index("expert") * 2 + lax.axis_index("sub")
    return me, me ^ 1


def route_kernel(
    live_ref, hidden_hbm, gain_hbm, router_hbm, ids_hbm, packet_ref, hidden_ref, gain_ref, router_ref, ids_ref, sems
):
    pairs = (
        (hidden_hbm, hidden_ref),
        (gain_hbm, gain_ref),
        (router_hbm, router_ref),
        (ids_hbm, ids_ref),
    )
    copies = [pltpu.make_async_copy(x, y, sems.at[i]) for i, (x, y) in enumerate(pairs)]
    for c in copies:
        c.start()
    for c in copies:
        c.wait()
    rows, width = hidden_ref.shape
    experts = router_ref.shape[0]
    lanes = packet_ref.shape[1] - width
    values = hidden_ref[...].astype(F32)
    spread = jnp.mean(values * values, axis=-1, keepdims=True)
    normed = (values * lax.rsqrt(spread + 1e-06) * gain_ref[...]).astype(BF16)
    packet_ref[:, :width] = normed
    logits = lax.dot_general(
        router_ref[...], normed, (((1,), (1,)), ((), ())), preferred_element_type=F32
    )
    probs = 1.0 / (1.0 + jnp.exp(-logits))
    live = (iota((1, rows), 1) < live_ref[0]).astype(F32)
    seats = iota((experts, rows), 0)
    named = jnp.zeros((experts, rows), F32)
    for k in range(ids_ref.shape[0]):
        named = named + (ids_ref[k : k + 1, :] == seats).astype(F32)
    picked = named * probs
    weights = (live * picked / jnp.sum(picked, axis=0, keepdims=True)).astype(BF16)
    taken = named * live
    earlier = (iota((rows, rows), 0) < iota((rows, rows), 1)).astype(F32).astype(BF16)
    slot = jnp.dot(taken.astype(BF16), earlier, preferred_element_type=F32)
    code = (taken * (slot + 1.0)).astype(BF16)
    load = jnp.sum(taken, axis=1, keepdims=True).astype(BF16)
    mass = jnp.sum(probs * live, axis=1, keepdims=True)
    meta = jnp.zeros((rows, lanes), F32)
    for at, piece in enumerate([weights, code, load, *split_three(mass)]):
        put = iota((experts, lanes), 1) == iota((experts, lanes), 0) + at * experts
        piece = jnp.broadcast_to(piece.astype(F32), (experts, rows)).astype(BF16)
        meta = meta + lax.dot_general(
            piece,
            put.astype(F32).astype(BF16),
            (((0,), (0,)), ((), ())),
            preferred_element_type=F32,
        )
    packet_ref[:, width:] = meta.astype(BF16)


def columns_of(block_ref, width, at):
    notes = block_ref[:, width:].astype(F32)
    lane = iota(notes.shape, 1)
    return [jnp.sum(jnp.where(lane == a, notes, 0.0), axis=1, keepdims=True) for a in at]


def matches(block_ref, width, experts, capacity):
    me, peer = my_seat()
    rows = block_ref.shape[0]
    mine, theirs = columns_of(block_ref, width, [experts + me, experts + peer])
    slot = iota((rows, 2 * capacity), 1)
    place = jnp.where(slot < capacity, mine, theirs).astype(jnp.int32)
    return (place - 1) == jnp.where(slot < capacity, slot, slot - capacity), slot


def pick_kernel(count, width, experts, capacity, *refs):
    blocks, (mine_ref, peer_ref) = refs[:count], refs[count:]
    sums = []
    for i, block in enumerate(blocks):
        match, _ = matches(block, width, experts, capacity)
        rows = lax.dot_general(
            match.astype(F32).astype(BF16),
            block[:, :width],
            (((0,), (0,)), ((), ())),
            preferred_element_type=F32,
        ).astype(BF16)
        mine_ref[i * capacity : (i + 1) * capacity, :] = rows[:capacity]
        peer_ref[i * capacity : (i + 1) * capacity, :] = rows[capacity:]
        sums.append(block[0:1, width:].astype(F32))
    filler = jnp.zeros((16 - count, sums[0].shape[1]), F32)
    sums = jnp.concatenate(sums + [filler], axis=0).astype(BF16)
    for ref in (mine_ref, peer_ref):
        ref[count * capacity :, : sums.shape[1]] = sums


def silu(value):
    return value / (1.0 + jnp.exp(-value))


def load_kernel(*refs):
    count = (len(refs) - 1) // 2
    sems = refs[-1]
    copies = [pltpu.make_async_copy(refs[i], refs[count + i], sems.at[i]) for i in range(count)]
    for c in copies:
        c.start()
    for c in copies:
        c.wait()


def expert_kernel(start, mine_ref, peer_ref, up_ref, down_ref, mine_out, peer_out, active):
    half, width = mine_out.shape
    units = down_ref.shape[0]
    end = start + half
    rows = jnp.concatenate([mine_ref[start:end, :], peer_ref[start:end, :]], axis=0)
    for at in range(0, units, 256):
        to = min(at + 256, units)
        gate = jnp.dot(rows, up_ref[:, at:to], preferred_element_type=F32)
        up = jnp.dot(rows, up_ref[:, units + at : units + to], preferred_element_type=F32)
        active[:, at:to] = (silu(gate) * up).astype(BF16)
    for at in range(0, width, 512):
        to = min(at + 512, width)
        result = jnp.dot(active[...], down_ref[:, at:to], preferred_element_type=F32).astype(BF16)
        mine_out[:, at:to] = result[:half]
        peer_out[:, at:to] = result[half:]


def shared_kernel(count, width, *refs):
    blocks, weights_ref, outs = refs[:count], refs[count], refs[count + 1 :]
    states = jnp.concatenate([b[:, :width] for b in blocks], axis=0)
    across = (((1,), (1,)), ((), ()))
    gate = lax.dot_general(states, weights_ref[0], across, preferred_element_type=F32)
    up = lax.dot_general(states, weights_ref[1], across, preferred_element_type=F32)
    active = (silu(gate) * up).astype(BF16)
    at = 0
    for out in outs:
        rows = active[at : at + out.shape[0]]
        out[...] = jnp.dot(rows, weights_ref[2], preferred_element_type=F32)
        at += out.shape[0]


def mix_kernel(count, width, experts, capacity, cuts, *refs):
    blocks, (mine_ref, peer_ref, shared_ref) = refs[:count], refs[count : count + 3]
    outs, at = [], count + 3
    for pieces in cuts:
        outs.append(refs[at : at + pieces])
        at += pieces
    me, peer = my_seat()
    rows = blocks[0].shape[0]
    for i, block in enumerate(blocks):
        match, slot = matches(block, width, experts, capacity)
        mine, theirs = columns_of(block, width, [me, peer])
        mixing = jnp.where(match, jnp.where(slot < capacity, mine, theirs), 0.0).astype(BF16)
        at = slice(i * capacity, (i + 1) * capacity)
        results = jnp.concatenate([mine_ref[at, :], peer_ref[at, :]], axis=0)
        total = shared_ref[i * rows : (i + 1) * rows, :] + jnp.dot(
            mixing, results, preferred_element_type=F32
        )
        at = 0
        for out in outs[i]:
            out[...] = total[:, at : at + out.shape[1]].astype(out.dtype)
            at += out.shape[1]


def add_kernel(keep_ref, more_ref, out_ref):
    out_ref[...] = (keep_ref[...] + more_ref[...].astype(F32)).astype(out_ref.dtype)


def sum_kernel(*refs):
    terms, out_ref = refs[:-1], refs[-1]
    width = out_ref.shape[1]
    narrow = min(term.shape[1] for term in terms)
    starts, at = [], 0
    for term in terms:
        starts.append(at)
        at = (at + term.shape[1]) % width
    for left in range(0, width, narrow):
        total = None
        for start, term in zip(starts, terms):
            if start <= left < start + term.shape[1]:
                piece = term[:, left - start : left - start + narrow].astype(F32)
                total = piece if total is None else total + piece
        out_ref[:, left : left + narrow] = total.astype(out_ref.dtype)


def penalty_kernel(experts, scale, steps, *refs):
    sums, out_ref = refs[:-1], refs[-1]
    own = jnp.concatenate([s[...] for s in sums[0::2]], axis=0)
    peer = jnp.concatenate([s[...] for s in sums[1::2]], axis=0)
    seats = own.shape[0]
    seat = lax.axis_index("expert")
    row = iota((seats, seats), 1)
    step = jnp.zeros_like(row)
    for r, k in enumerate(steps):
        step = jnp.where(row == r, k, step)
    order = (iota((seats, seats), 0) == (step ^ seat)).astype(F32).astype(BF16)
    own = jnp.dot(order, own, preferred_element_type=F32)
    peer = jnp.dot(order, peer, preferred_element_type=F32)

    def part(array, i):
        return array[:, i * experts : (i + 1) * experts]

    load = jnp.sum(part(own, 2) + part(peer, 2), axis=0, keepdims=True)
    mass = (part(own, 3) + part(own, 4) + part(own, 5)) + (part(peer, 3) + part(peer, 4) + part(peer, 5))
    mass = jnp.sum(mass, axis=0, keepdims=True)
    out_ref[...] = jnp.sum(load * mass, axis=1, keepdims=True) * experts / scale


def call(kernel, out_shape, where, flops, nbytes, mib, scratch=(), out="v"):
    spaces = {"v": pltpu.VMEM, "s": pltpu.SMEM, "h": pltpu.HBM}
    many = isinstance(out_shape, (list, tuple))
    specs = {"v": VMEM, "s": SMEM, "h": pl.BlockSpec(memory_space=pltpu.HBM)}

    def vmem(x):
        return pltpu.VMEM(x.shape, x.dtype) if out == "v" else x

    run = pl.pallas_call(
        kernel,
        out_shape=[vmem(x) for x in out_shape] if many else vmem(out_shape),
        in_specs=[specs[w] for w in where],
        out_specs=[VMEM] * len(out_shape) if many else VMEM,
        scratch_shapes=list(scratch),
        cost_estimate=pl.CostEstimate(flops=flops, bytes_accessed=nbytes, transcendentals=0),
        compiler_params=pltpu.CompilerParams(vmem_limit_bytes=mib << 20),
    )

    def go(*args):
        args = [
            a if w == "s" else pltpu.with_memory_space_constraint(a, spaces[w])
            for a, w in zip(args, where)
        ]
        return run(*args)

    return go


def chunks_of(steps):
    return [[0], list(range(2, steps, 2)), list(range(3, steps, 2)) + [1]]


def parts_of(chunk):
    return [chunk[:-1], chunk[-1:]] if len(chunk) > 1 and chunk[-1] == 1 else [chunk]


def pieces_of(step, steps):
    return 2 if step == steps - 1 else 1


def on_device(
    hidden_state,
    norm_gain,
    router_weight,
    expert_ids,
    live_counts,
    routed_gate_up,
    routed_down,
    shared_weights,
):
    tok_rows, width = hidden_state.shape
    choose = expert_ids.shape[1]
    hidden_units = routed_down.shape[1]
    expert_count = lax.axis_size("expert")
    sub_count = lax.axis_size("sub")
    devices = expert_count * sub_count
    all_experts = routed_gate_up.shape[0] * devices
    assert routed_gate_up.shape[0] == 1 and sub_count == 2
    all_tokens = tok_rows * devices
    capacity = (tok_rows * choose * 4 + 3 * all_experts - 1) // (3 * all_experts)
    shape = jax.ShapeDtypeStruct

    def cross(block, step):
        return lax.ppermute(block, "expert", [(e, e ^ step) for e in range(expert_count)])

    def swap(block):
        return lax.ppermute(block, "sub", [(0, 1), (1, 0)])

    lanes = -(-6 * all_experts // 128) * 128
    packet = call(
        route_kernel,
        shape((tok_rows, width + lanes), BF16),
        "shhhh",
        2 * tok_rows * width * all_experts,
        4 * tok_rows * width,
        8,
        [
            pltpu.VMEM((tok_rows, width), BF16),
            pltpu.VMEM((1, width), F32),
            pltpu.VMEM((all_experts, width), BF16),
            pltpu.VMEM((choose, tok_rows), jnp.int32),
            pltpu.SemaphoreType.DMA((4,)),
        ],
    )(live_counts, hidden_state, norm_gain.reshape(1, width), router_weight.T, expert_ids.T)

    steps = expert_count // 2
    chunks = chunks_of(steps)
    direct = [packet, cross(packet, 2)]
    for j in range(2, steps):
        direct.append(cross(direct[j - 1], 2) if j % 2 else cross(packet, 2 * j))
    near = []
    for j in range(steps):
        far = j > 1 and j % 2
        near.append(cross(near[j - 1], 2) if far else cross(direct[j], 1))

    def load(*arrays):
        return call(
            load_kernel,
            [shape(a.shape, a.dtype) for a in arrays],
            "h" * len(arrays),
            0,
            sum(2 * a.size for a in arrays),
            1,
            [pltpu.SemaphoreType.DMA((len(arrays),))],
        )(*arrays)

    (gate_up,) = load(routed_gate_up[0])
    down, shared_rows = load(routed_down[0], jnp.swapaxes(shared_weights, 1, 2))
    arrived = [(direct[j], near[j]) for j in range(steps)]

    keeps, leaves, sums = [None] * steps, [None] * steps, []
    for chunk in chunks:
        blocks = [b for j in chunk for b in arrived[j]]
        count = len(blocks)
        picked = shape((count * capacity + 16, width), BF16)
        mine, theirs = call(
            functools.partial(pick_kernel, count, width, all_experts, capacity),
            (picked, picked),
            "v" * count,
            4 * count * tok_rows * capacity * width,
            8 * count * capacity * width,
            8,
        )(*blocks)
        theirs = swap(theirs)
        sums += [x[count * capacity :][:count, :lanes] for x in (mine, theirs)]
        parts = parts_of(chunk)
        shared = call(
            functools.partial(shared_kernel, count, width),
            [shape((2 * len(steps_in) * tok_rows, width), F32) for steps_in in parts],
            "v" * (count + 1),
            6 * count * tok_rows * width * shared_rows.shape[1],
            6 * width * shared_rows.shape[1],
            8,
        )(*blocks, shared_rows)
        at = 0
        for steps_in, extra in zip(parts, shared):
            count = 2 * len(steps_in)
            results = shape((count * capacity, width), BF16)
            here, away = call(
                functools.partial(expert_kernel, at * capacity),
                (results, results),
                "vvvv",
                12 * count * capacity * width * hidden_units,
                6 * width * hidden_units,
                8,
                [pltpu.VMEM((2 * count * capacity, hidden_units), BF16)],
            )(mine, theirs, gate_up, down)
            away = swap(away)
            cuts = [pieces_of(j, steps) for j in steps_in for _ in range(2)]
            kinds = [F32, BF16] * len(steps_in)
            totals = call(
                functools.partial(mix_kernel, count, width, all_experts, capacity, cuts),
                [shape((tok_rows, width // n), t) for n, t in zip(cuts, kinds) for _ in range(n)],
                "v" * (count + 3),
                4 * count * tok_rows * capacity * width,
                8 * count * tok_rows * width,
                8,
            )(*blocks[at : at + count], here, away, extra)
            for j in steps_in:
                n = pieces_of(j, steps)
                keeps[j], leaves[j], totals = totals[:n], totals[n : 2 * n], totals[2 * n :]
            at = at + count

    terms = [keeps[0][0], cross(leaves[0][0], 1)]
    for j in range(1, steps):
        for keep, leave in zip(keeps[j], leaves[j]):
            more = cross(leave, 1)
            both = call(add_kernel, shape(keep.shape, BF16), "vv", 0, 0, 4)(keep, more)
            terms.append(cross(both, 2 * j))
    mixed = call(sum_kernel, shape((tok_rows, width), BF16), "v" * len(terms), 0, 0, 8, out="h")(*terms)

    penalty = call(
        functools.partial(
            penalty_kernel,
            all_experts,
            choose * float(all_tokens) * float(all_tokens),
            [2 * j + b for chunk in chunks for j in chunk for b in range(2)],
        ),
        shape((1, 1), F32),
        "v" * len(sums),
        0,
        0,
        4,
    )(*sums)
    return (mixed, penalty.reshape(1))


def solution(mesh):
    placed = (
        P(("groups", "expert", "sub"), None),
        P(),
        P(),
        P(("groups", "expert", "sub"), None),
        P(("groups", "expert", "sub")),
        P(("expert", "sub"), None, None),
        P(("expert", "sub"), None, None),
        P(None, None, "expert"),
    )

    return jax.shard_map(
        on_device,
        mesh=mesh,
        in_specs=placed,
        out_specs=(P(("groups", "expert", "sub"), None), P("groups")),
        check_vma=False,
    )
```
